256 devices in a mesh: rows: 8 (over y, core), cols: 32 (over z, x).
Axes of the slice: x: 4, y: 4, z: 8, core: 2. Of those that a mesh axis runs over, the one named last changes fastest.
Arguments:
- kernel: float32 [8192, 65536], P('rows', 'cols'), may hold values from -0.09375 to 0.09375
- slip_delta: float32 [64, 32, 128], P('cols', 'rows'), may hold values from -6 to 6
- block_list: int32 [64, 32], P('cols', 'rows'), may hold values from 0 to 511, as said below
- live_count: int32 [64], P('cols'), may hold values from 1 to 32, 1024 in all
- direct_effect: float32 [8192], P(('rows', 'cols')), may hold values from 0.5 to 2
- load_rate: float32 [8192], P(('rows', 'cols')), may hold values from 0.02 to 0.2
- time_before: float32 [8192], P(('rows', 'cols')), may hold values from 1 to 50
Outputs:
- stress_change: float32 [8192, 64], P(('rows', 'cols'))
- log_time: float32 [8192, 64], P(('rows', 'cols'))
The draws below stay inside these ranges and needn't reach their ends.
Inputs may be any that keep to these rules, and one draw needn't show every extreme that they name: The first live_count[e] entries of row e of block_list are distinct block numbers; the rest of the row are padding.
All inputs are finite; a program needn't handle non-finite values. No bound on the sum of `live_count` on one device may be relied on, other than what follows from the above.
Results may differ from the reference program's by a relative error of at most 0.00007.
Values sent between devices are 32-bit elements; how exact they have to be, the bound alone decides.
A program may use at most 64 MiB of HBM per device.

```python
import math
import jax
import jax.numpy as jnp
import numpy as np
from jax import lax

BLOCK = 128
EVENTS = 64
LIST = 32
NR = 8192
NB = 512
NS = 65536


def draw_block_list(key, part):
    event_keys = jax.random.split(jax.random.fold_in(key, 11), EVENTS)
    shuffled = jax.vmap(lambda k: jax.random.permutation(k, NB))(event_keys)[:, :LIST].astype(jnp.int32)
    inner = jax.random.permutation(jax.random.fold_in(key, 12), NB - 2)[:LIST - 2].astype(jnp.int32) + 1
    first_row = jnp.concatenate([jnp.array([0, NB - 1], jnp.int32), inner])
    first_row = jax.random.permutation(jax.random.fold_in(key, 13), first_row).astype(jnp.int32)
    return shuffled.at[0].set(first_row)


def steps_of(own_key, extent, cuts, low, top_value):
    loudness = 1.0
    for dim, shards_of in cuts:
        draws = jax.random.uniform(jax.random.fold_in(jax.random.fold_in(own_key, 6), dim), (shards_of,), jnp.float32, low / len(cuts), top_value / len(cuts))
        loudness = loudness * jnp.repeat(jnp.exp(draws), extent[dim] // shards_of).reshape((-1,) + (1,) * (len(extent) - 1 - dim))
    return loudness


def profile(count, total, limit, skew):
    weights = [(1 << 20) // math.isqrt(standing ** skew) + 1 for standing in range(2, count + 1)]
    surplus, holding = total - limit - (count - 1), [1] * (count - 1)
    while surplus > 0:
        candidates = [i for i in range(count - 1) if holding[i] < limit]
        whole, left = sum([weights[i] for i in candidates]), surplus
        for i in candidates:
            addition = min(limit - holding[i], max(1, left * weights[i] // whole), surplus)
            holding[i] = holding[i] + addition
            surplus = surplus - addition
    return np.array([limit] + holding)


def uneven(rng, number_of, total, most, lean):
    if number_of == 2:
        one = jax.random.randint(rng, (), max(1, total - most), min(most, total - 1) + 1)
        return jnp.stack([one, total - one])
    tallies = jnp.asarray(profile(number_of, total, most, lean), jnp.int32)
    twos = (number_of - 1) // 2
    source_of, sink = tallies[1:1 + 2 * twos:2], tallies[2:2 + 2 * twos:2]
    room = jnp.minimum(source_of - 1, most - sink)
    shifted = jax.random.randint(jax.random.fold_in(rng, 1), (twos,), 0, 1 << 20) % (room + 1)
    tallies = tallies.at[1:1 + 2 * twos:2].set(source_of - shifted).at[2:2 + 2 * twos:2].set(sink + shifted)
    return tallies[jax.random.permutation(jax.random.fold_in(rng, 2), number_of)]


def bell_draw(own_key, extent, spread, most, shards=(), kind=jnp.bfloat16):
    loudness = steps_of(own_key, extent, shards, -0.22, 0.18) if shards else 1.0
    values = jax.random.normal(own_key, extent, jnp.float32) * spread * loudness
    return jnp.minimum(jnp.maximum(values, -most), most).astype(kind)


def setup_inputs(seed: int = 0) -> dict:
    seeds = jax.random.split(jax.random.key(seed), 8)
    kernel = bell_draw(seeds[0], (NR, NS), (LIST * BLOCK) ** -0.5, 0.09375, ((0, 8), (1, 32)), jnp.float32)
    slip_delta = bell_draw(seeds[1], (EVENTS, LIST, BLOCK), 1.0, 6.0, ((0, 32), (1, 8)), jnp.float32)
    block_list = draw_block_list(jax.random.fold_in(seeds[7], 71), 0)
    live_count = uneven(seeds[3], EVENTS, EVENTS * LIST // 2, LIST, 2).astype(jnp.int32)
    direct_effect = jnp.clip(jnp.exp(math.log(2.0) - 1.3862944 * jax.random.uniform(seeds[4], (NR,), jnp.float32) ** steps_of(seeds[4], (NR,), ((0, 256),), -0.2, 0.2)), 0.5, 2.0)
    load_rate = jnp.clip(jnp.exp(math.log(0.2) - 2.3025851 * jax.random.uniform(seeds[5], (NR,), jnp.float32) ** steps_of(seeds[5], (NR,), ((0, 256),), -0.2, 0.2)), 0.02, 0.2)
    time_before = jnp.clip(jnp.exp(math.log(50.0) - 3.912023 * jax.random.uniform(seeds[6], (NR,), jnp.float32) ** steps_of(seeds[6], (NR,), ((0, 256),), -0.2, 0.2)), 1.0, 50.0)
    return dict(kernel=kernel, slip_delta=slip_delta, block_list=block_list, live_count=live_count, direct_effect=direct_effect, load_rate=load_rate, time_before=time_before)


def reference(kernel, slip_delta, block_list, live_count, direct_effect, load_rate, time_before):
    live_mask = (jnp.arange(LIST, dtype=jnp.int32)[None, :] < live_count[:, None]).astype(jnp.float32)
    event_rows = jnp.broadcast_to(jnp.arange(EVENTS, dtype=jnp.int32)[:, None], (EVENTS, LIST))
    dense_slip = jnp.zeros((EVENTS, NB, BLOCK), jnp.float32)
    dense_slip = dense_slip.at[event_rows, block_list].add(slip_delta * live_mask[:, :, None])
    dense_slip = dense_slip.reshape(EVENTS, NS)
    stress_change = lax.dot_general(kernel, dense_slip, (((1,), (1,)), ((), ())), precision=lax.Precision.HIGHEST, preferred_element_type=jnp.float32)
    scale = direct_effect[:, None]
    growth = jnp.expm1(load_rate * time_before / direct_effect)[:, None]
    log_time = jnp.log(scale / load_rate[:, None]) + jnp.log(jnp.log1p(jnp.exp(-stress_change / scale) * growth))
    return stress_change, log_time
```

```python
import functools

import jax
import jax.numpy as jnp
from jax import lax
from jax.experimental import pallas as pl
from jax.experimental.pallas import tpu as pltpu
from jax.sharding import PartitionSpec as P

BLOCK = 128
MESH = pl.DeviceIdType.MESH


def scatter_sum_kernel(ncols, part_ref, out_ref, slots, send_sem, recv_sem):
    me = lax.axis_index("cols")
    row = lax.axis_index("rows")
    share = out_ref.shape[0]

    barrier = pltpu.get_barrier_semaphore()
    for k in range(1, ncols):
        peer = lax.rem(me + k, ncols)
        pl.semaphore_signal(barrier, inc=1, device_id=(row, peer), device_id_type=MESH)
    pl.semaphore_wait(barrier, ncols - 1)

    copies = []
    for k in range(1, ncols):
        peer = lax.rem(me + k, ncols)
        copy = pltpu.make_async_remote_copy(
            src_ref=part_ref.at[pl.ds(pl.multiple_of(peer * share, share), share)],
            dst_ref=slots.at[me],
            send_sem=send_sem.at[peer],
            recv_sem=recv_sem.at[me],
            device_id=(row, peer),
            device_id_type=MESH,
        )
        copy.start()
        copies.append(copy)

    total = part_ref[pl.ds(pl.multiple_of(me * share, share), share), :]
    for k in range(1, ncols):
        src = lax.rem(me + ncols - k, ncols)
        pltpu.make_async_remote_copy(
            src_ref=part_ref.at[pl.ds(0, share)],
            dst_ref=slots.at[src],
            send_sem=send_sem.at[src],
            recv_sem=recv_sem.at[src],
            device_id=(row, src),
            device_id_type=MESH,
        ).wait_recv()
        total = total + slots[src]
    out_ref[...] = total
    for copy in copies:
        copy.wait_send()


def scatter_sum(partial, ncols):
    rows, events = partial.shape
    share = rows // ncols
    return pl.pallas_call(
        functools.partial(scatter_sum_kernel, ncols),
        out_shape=jax.ShapeDtypeStruct((share, events), jnp.float32),
        in_specs=[pl.BlockSpec(memory_space=pltpu.VMEM)],
        out_specs=pl.BlockSpec(memory_space=pltpu.VMEM),
        scratch_shapes=[
            pltpu.VMEM((ncols, share, events), jnp.float32),
            pltpu.SemaphoreType.DMA((ncols,)),
            pltpu.SemaphoreType.DMA((ncols,)),
        ],
        compiler_params=pltpu.CompilerParams(collective_id=0, has_side_effects=True),
    )(partial)


def exchange_kernel(axis, other_axis, n, same, x_ref, out_ref, slots, send_sem, recv_sem):
    me = lax.axis_index(axis)
    other = lax.axis_index(other_axis)

    def device(peer):
        return (other, peer) if axis == "cols" else (peer, other)

    barrier = pltpu.get_barrier_semaphore()
    for k in range(1, n):
        peer = lax.rem(me + k, n)
        pl.semaphore_signal(barrier, inc=1, device_id=device(peer), device_id_type=MESH)
    pl.semaphore_wait(barrier, n - 1)

    copies = []
    for k in range(1, n):
        peer = lax.rem(me + k, n)
        copy = pltpu.make_async_remote_copy(
            src_ref=x_ref if same else x_ref.at[peer],
            dst_ref=slots.at[me],
            send_sem=send_sem.at[peer],
            recv_sem=recv_sem.at[me],
            device_id=device(peer),
            device_id_type=MESH,
        )
        copy.start()
        copies.append(copy)

    out_ref[me] = x_ref[...] if same else x_ref[me]
    for k in range(1, n):
        src = lax.rem(me + n - k, n)
        pltpu.make_async_remote_copy(
            src_ref=x_ref if same else x_ref.at[src],
            dst_ref=slots.at[src],
            send_sem=send_sem.at[src],
            recv_sem=recv_sem.at[src],
            device_id=device(src),
            device_id_type=MESH,
        ).wait_recv()
        out_ref[src] = slots[src]
    for copy in copies:
        copy.wait_send()


def exchange(x, axis, other_axis, n, same, collective_id):
    chunk = x.shape if same else x.shape[1:]
    return pl.pallas_call(
        functools.partial(exchange_kernel, axis, other_axis, n, same),
        out_shape=jax.ShapeDtypeStruct((n,) + chunk, x.dtype),
        in_specs=[pl.BlockSpec(memory_space=pltpu.VMEM)],
        out_specs=pl.BlockSpec(memory_space=pltpu.VMEM),
        scratch_shapes=[
            pltpu.VMEM((n,) + chunk, x.dtype),
            pltpu.SemaphoreType.DMA((n,)),
            pltpu.SemaphoreType.DMA((n,)),
        ],
        compiler_params=pltpu.CompilerParams(
            collective_id=collective_id, has_side_effects=True
        ),
    )(x)


def per_device(kernel, slip_delta, block_list, live_count, direct_effect, load_rate, time_before):
    nrows = lax.axis_size("rows")
    ncols = lax.axis_size("cols")
    my_row = lax.axis_index("rows")
    events_here, list_here, _ = slip_delta.shape
    blocks = kernel.shape[1] // BLOCK
    entry = my_row * list_here + jnp.arange(list_here, dtype=jnp.int32)
    live = entry[None, :] < live_count[:, None]
    key = jnp.where(live, block_list, -1).astype(jnp.float32)
    payload = jnp.stack(
        [slip_delta, jnp.broadcast_to(key[:, :, None], slip_delta.shape)], axis=0
    )
    gathered = exchange(payload, "rows", "cols", nrows, True, 1)
    gathered = jnp.moveaxis(gathered, 0, 2).reshape(2, events_here, nrows * list_here, BLOCK)
    slip_full = gathered[0]
    key_full = gathered[1][:, :, 0].astype(jnp.int32)
    total_blocks = blocks * ncols
    onehot = (
        key_full[:, :, None] == jnp.arange(total_blocks, dtype=jnp.int32)[None, None, :]
    ).astype(jnp.float32)
    dense_own = jnp.einsum("ebj,ebc->ejc", onehot, slip_full, precision=lax.Precision.HIGHEST)
    dense_own = dense_own.reshape(events_here, ncols, blocks * BLOCK)
    dense_own = jnp.moveaxis(dense_own, 1, 0)
    dense_slip = exchange(dense_own, "cols", "rows", ncols, False, 2)
    dense_slip = dense_slip.reshape(ncols * events_here, blocks * BLOCK)
    partial_sum = lax.dot_general(
        kernel,
        dense_slip,
        (((1,), (1,)), ((), ())),
        precision=lax.Precision.HIGHEST,
        preferred_element_type=jnp.float32,
    )
    stress_change = scatter_sum(partial_sum, ncols)
    scale = direct_effect[:, None]
    growth = jnp.expm1(load_rate * time_before / direct_effect)[:, None]
    log_time = jnp.log(scale / load_rate[:, None]) + jnp.log(
        jnp.log1p(jnp.exp(-stress_change / scale) * growth)
    )
    return (stress_change, log_time)


def solution(mesh):
    in_specs = (
        P("rows", "cols"),
        P("cols", "rows", None),
        P("cols", "rows"),
        P("cols"),
        P(("rows", "cols")),
        P(("rows", "cols")),
        P(("rows", "cols")),
    )
    out_specs = (P(("rows", "cols"), None), P(("rows", "cols"), None))
    return jax.shard_map(
        per_device, mesh=mesh, in_specs=in_specs, out_specs=out_specs, check_vma=False
    )
```

```python
import functools

import jax
import jax.numpy as jnp
from jax import lax
from jax.experimental import pallas as pl
from jax.experimental.pallas import tpu as pltpu
from jax.sharding import PartitionSpec as P

BLOCK = 128
MESH = pl.DeviceIdType.MESH


def stress_kernel(ncols, groups, kernel_ref, dense_ref, out_ref, sendbuf, slots, send_sem, recv_sem):
    me = lax.axis_index("cols")
    row = lax.axis_index("rows")
    share = out_ref.shape[0]
    per_group = ncols // groups

    barrier = pltpu.get_barrier_semaphore()
    for k in range(1, ncols):
        peer = lax.rem(me + k, ncols)
        pl.semaphore_signal(barrier, inc=1, device_id=(row, peer), device_id_type=MESH)

    copies = []
    for g in range(groups):
        first = lax.rem(me + 1 + g * per_group, ncols)
        for j in range(per_group):
            dest = lax.rem(first + j, ncols)
            rows = pl.ds(pl.multiple_of(dest * share, share), share)
            sendbuf[dest] = lax.dot_general(
                kernel_ref[rows, :],
                dense_ref[...],
                (((1,), (1,)), ((), ())),
                precision=lax.Precision.HIGHEST,
                preferred_element_type=jnp.float32,
            )
        if g == 0:
            pl.semaphore_wait(barrier, ncols - 1)
        for j in range(per_group):
            k = 1 + g * per_group + j
            if k == ncols:
                continue
            dest = lax.rem(me + k, ncols)
            copy = pltpu.make_async_remote_copy(
                src_ref=sendbuf.at[dest],
                dst_ref=slots.at[me],
                send_sem=send_sem.at[dest],
                recv_sem=recv_sem.at[me],
                device_id=(row, dest),
                device_id_type=MESH,
            )
            copy.start()
            copies.append(copy)

    total = sendbuf[me]
    for k in range(1, ncols):
        src = lax.rem(me + ncols - k, ncols)
        pltpu.make_async_remote_copy(
            src_ref=sendbuf.at[src],
            dst_ref=slots.at[src],
            send_sem=send_sem.at[src],
            recv_sem=recv_sem.at[src],
            device_id=(row, src),
            device_id_type=MESH,
        ).wait_recv()
        total = total + slots[src]
    out_ref[...] = total
    for copy in copies:
        copy.wait_send()


def stress_sum(kernel, dense, ncols, groups=4):
    rows = kernel.shape[0]
    events = dense.shape[0]
    share = rows // ncols
    return pl.pallas_call(
        functools.partial(stress_kernel, ncols, groups),
        out_shape=jax.ShapeDtypeStruct((share, events), jnp.float32),
        in_specs=[pl.BlockSpec(memory_space=pltpu.VMEM)] * 2,
        out_specs=pl.BlockSpec(memory_space=pltpu.VMEM),
        scratch_shapes=[
            pltpu.VMEM((ncols, share, events), jnp.float32),
            pltpu.VMEM((ncols, share, events), jnp.float32),
            pltpu.SemaphoreType.DMA((ncols,)),
            pltpu.SemaphoreType.DMA((ncols,)),
        ],
        compiler_params=pltpu.CompilerParams(
            collective_id=0, has_side_effects=True, vmem_limit_bytes=40 * 1024 * 1024
        ),
    )(kernel, dense)


def exchange_kernel(axis, other_axis, n, same, x_ref, out_ref, slots, send_sem, recv_sem):
    me = lax.axis_index(axis)
    other = lax.axis_index(other_axis)

    def device(peer):
        return (other, peer) if axis == "cols" else (peer, other)

    barrier = pltpu.get_barrier_semaphore()
    for k in range(1, n):
        peer = lax.rem(me + k, n)
        pl.semaphore_signal(barrier, inc=1, device_id=device(peer), device_id_type=MESH)
    pl.semaphore_wait(barrier, n - 1)

    copies = []
    for k in range(1, n):
        peer = lax.rem(me + k, n)
        copy = pltpu.make_async_remote_copy(
            src_ref=x_ref if same else x_ref.at[peer],
            dst_ref=slots.at[me],
            send_sem=send_sem.at[peer],
            recv_sem=recv_sem.at[me],
            device_id=device(peer),
            device_id_type=MESH,
        )
        copy.start()
        copies.append(copy)

    out_ref[me] = x_ref[...] if same else x_ref[me]
    for k in range(1, n):
        src = lax.rem(me + n - k, n)
        pltpu.make_async_remote_copy(
            src_ref=x_ref if same else x_ref.at[src],
            dst_ref=slots.at[src],
            send_sem=send_sem.at[src],
            recv_sem=recv_sem.at[src],
            device_id=device(src),
            device_id_type=MESH,
        ).wait_recv()
        out_ref[src] = slots[src]
    for copy in copies:
        copy.wait_send()


def exchange(x, axis, other_axis, n, same, collective_id):
    chunk = x.shape if same else x.shape[1:]
    return pl.pallas_call(
        functools.partial(exchange_kernel, axis, other_axis, n, same),
        out_shape=jax.ShapeDtypeStruct((n,) + chunk, x.dtype),
        in_specs=[pl.BlockSpec(memory_space=pltpu.VMEM)],
        out_specs=pl.BlockSpec(memory_space=pltpu.VMEM),
        scratch_shapes=[
            pltpu.VMEM((n,) + chunk, x.dtype),
            pltpu.SemaphoreType.DMA((n,)),
            pltpu.SemaphoreType.DMA((n,)),
        ],
        compiler_params=pltpu.CompilerParams(
            collective_id=collective_id, has_side_effects=True
        ),
    )(x)


def per_device(kernel, slip_delta, block_list, live_count, direct_effect, load_rate, time_before):
    nrows = lax.axis_size("rows")
    ncols = lax.axis_size("cols")
    my_row = lax.axis_index("rows")
    events_here, list_here, _ = slip_delta.shape
    blocks = kernel.shape[1] // BLOCK
    entry = my_row * list_here + jnp.arange(list_here, dtype=jnp.int32)
    live = entry[None, :] < live_count[:, None]
    key = jnp.where(live, block_list, -1).astype(jnp.float32)
    payload = jnp.stack(
        [slip_delta, jnp.broadcast_to(key[:, :, None], slip_delta.shape)], axis=0
    )
    gathered = exchange(payload, "rows", "cols", nrows, True, 1)
    gathered = jnp.moveaxis(gathered, 0, 2).reshape(2, events_here, nrows * list_here, BLOCK)
    slip_full = gathered[0]
    key_full = gathered[1][:, :, 0].astype(jnp.int32)
    total_blocks = blocks * ncols
    onehot = (
        key_full[:, :, None] == jnp.arange(total_blocks, dtype=jnp.int32)[None, None, :]
    ).astype(jnp.float32)
    dense_own = jnp.einsum("ebj,ebc->ejc", onehot, slip_full, precision=lax.Precision.HIGHEST)
    dense_own = dense_own.reshape(events_here, ncols, blocks * BLOCK)
    dense_own = jnp.moveaxis(dense_own, 1, 0)
    dense_slip = exchange(dense_own, "cols", "rows", ncols, False, 2)
    dense_slip = dense_slip.reshape(ncols * events_here, blocks * BLOCK)
    stress_change = stress_sum(kernel, dense_slip, ncols)
    scale = direct_effect[:, None]
    growth = jnp.expm1(load_rate * time_before / direct_effect)[:, None]
    log_time = jnp.log(scale / load_rate[:, None]) + jnp.log(
        jnp.log1p(jnp.exp(-stress_change / scale) * growth)
    )
    return (stress_change, log_time)


def solution(mesh):
    in_specs = (
        P("rows", "cols"),
        P("cols", "rows", None),
        P("cols", "rows"),
        P("cols"),
        P(("rows", "cols")),
        P(("rows", "cols")),
        P(("rows", "cols")),
    )
    out_specs = (P(("rows", "cols"), None), P(("rows", "cols"), None))
    return jax.shard_map(
        per_device, mesh=mesh, in_specs=in_specs, out_specs=out_specs, check_vma=False
    )
```

```python
import functools

import jax
import jax.numpy as jnp
from jax import lax
from jax.experimental import pallas as pl
from jax.experimental.pallas import tpu as pltpu
from jax.sharding import PartitionSpec as P

BLOCK = 128
MESH = pl.DeviceIdType.MESH


def stress_kernel(ncols, groups, own_ref, kernel_hbm, out_ref, kmat, dense, sendbuf, slots, kload_sem, local_sem, a_send, a_recv, send_sem, recv_sem):
    me = lax.axis_index("cols")
    row = lax.axis_index("rows")
    share = out_ref.shape[0]
    per_group = ncols // groups
    here = own_ref.shape[1]
    quarter = kmat.shape[0] // 4

    loads = []
    for q in range(4):
        load = pltpu.make_async_copy(
            kernel_hbm.at[pl.ds(q * quarter, quarter)], kmat.at[pl.ds(q * quarter, quarter)], kload_sem.at[q]
        )
        load.start()
        loads.append(load)

    barrier = pltpu.get_barrier_semaphore()
    for k in range(1, ncols):
        peer = lax.rem(me + k, ncols)
        pl.semaphore_signal(barrier, inc=1, device_id=(row, peer), device_id_type=MESH)
    pl.semaphore_wait(barrier, ncols - 1)

    sends = []
    for k in range(1, ncols):
        peer = lax.rem(me + k, ncols)
        copy = pltpu.make_async_remote_copy(
            src_ref=own_ref.at[peer],
            dst_ref=dense.at[pl.ds(me * here, here)],
            send_sem=a_send.at[peer],
            recv_sem=a_recv.at[me],
            device_id=(row, peer),
            device_id_type=MESH,
        )
        copy.start()
        sends.append(copy)
    local = pltpu.make_async_copy(own_ref.at[me], dense.at[pl.ds(me * here, here)], local_sem)
    local.start()
    local.wait()
    for k in range(1, ncols):
        src = lax.rem(me + ncols - k, ncols)
        pltpu.make_async_remote_copy(
            src_ref=own_ref.at[src],
            dst_ref=dense.at[pl.ds(src * here, here)],
            send_sem=a_send.at[src],
            recv_sem=a_recv.at[src],
            device_id=(row, src),
            device_id_type=MESH,
        ).wait_recv()
    for load in loads:
        load.wait()

    for g in range(groups):
        first = lax.rem(me + 1 + g * per_group, ncols)
        for j in range(per_group):
            dest = lax.rem(first + j, ncols)
            rows = pl.ds(pl.multiple_of(dest * share, share), share)
            sendbuf[dest] = lax.dot_general(
                kmat[rows, :],
                dense[...],
                (((1,), (1,)), ((), ())),
                precision=lax.Precision.HIGHEST,
                preferred_element_type=jnp.float32,
            )
        for j in range(per_group):
            k = 1 + g * per_group + j
            if k == ncols:
                continue
            dest = lax.rem(me + k, ncols)
            copy = pltpu.make_async_remote_copy(
                src_ref=sendbuf.at[dest],
                dst_ref=slots.at[me],
                send_sem=send_sem.at[dest],
                recv_sem=recv_sem.at[me],
                device_id=(row, dest),
                device_id_type=MESH,
            )
            copy.start()
            sends.append(copy)

    total = sendbuf[me]
    for k in range(1, ncols):
        src = lax.rem(me + ncols - k, ncols)
        pltpu.make_async_remote_copy(
            src_ref=sendbuf.at[src],
            dst_ref=slots.at[src],
            send_sem=send_sem.at[src],
            recv_sem=recv_sem.at[src],
            device_id=(row, src),
            device_id_type=MESH,
        ).wait_recv()
        total = total + slots[src]
    out_ref[...] = total
    for copy in sends:
        copy.wait_send()


def stress_sum(kernel, dense_own, ncols, groups=4):
    rows, sources = kernel.shape
    here = dense_own.shape[1]
    events = ncols * here
    share = rows // ncols
    return pl.pallas_call(
        functools.partial(stress_kernel, ncols, groups),
        out_shape=jax.ShapeDtypeStruct((share, events), jnp.float32),
        in_specs=[pl.BlockSpec(memory_space=pltpu.VMEM), pl.BlockSpec(memory_space=pl.ANY)],
        out_specs=pl.BlockSpec(memory_space=pltpu.VMEM),
        scratch_shapes=[
            pltpu.VMEM((rows, sources), jnp.float32),
            pltpu.VMEM((events, sources), jnp.float32),
            pltpu.VMEM((ncols, share, events), jnp.float32),
            pltpu.VMEM((ncols, share, events), jnp.float32),
            pltpu.SemaphoreType.DMA((4,)),
            pltpu.SemaphoreType.DMA,
            pltpu.SemaphoreType.DMA((ncols,)),
            pltpu.SemaphoreType.DMA((ncols,)),
            pltpu.SemaphoreType.DMA((ncols,)),
            pltpu.SemaphoreType.DMA((ncols,)),
        ],
        compiler_params=pltpu.CompilerParams(
            collective_id=0, has_side_effects=True, vmem_limit_bytes=40 * 1024 * 1024
        ),
    )(dense_own, kernel)


def exchange_kernel(axis, other_axis, n, same, x_ref, out_ref, slots, send_sem, recv_sem):
    me = lax.axis_index(axis)
    other = lax.axis_index(other_axis)

    def device(peer):
        return (other, peer) if axis == "cols" else (peer, other)

    barrier = pltpu.get_barrier_semaphore()
    for k in range(1, n):
        peer = lax.rem(me + k, n)
        pl.semaphore_signal(barrier, inc=1, device_id=device(peer), device_id_type=MESH)
    pl.semaphore_wait(barrier, n - 1)

    copies = []
    for k in range(1, n):
        peer = lax.rem(me + k, n)
        copy = pltpu.make_async_remote_copy(
            src_ref=x_ref if same else x_ref.at[peer],
            dst_ref=slots.at[me],
            send_sem=send_sem.at[peer],
            recv_sem=recv_sem.at[me],
            device_id=device(peer),
            device_id_type=MESH,
        )
        copy.start()
        copies.append(copy)

    out_ref[me] = x_ref[...] if same else x_ref[me]
    for k in range(1, n):
        src = lax.rem(me + n - k, n)
        pltpu.make_async_remote_copy(
            src_ref=x_ref if same else x_ref.at[src],
            dst_ref=slots.at[src],
            send_sem=send_sem.at[src],
            recv_sem=recv_sem.at[src],
            device_id=device(src),
            device_id_type=MESH,
        ).wait_recv()
        out_ref[src] = slots[src]
    for copy in copies:
        copy.wait_send()


def exchange(x, axis, other_axis, n, same, collective_id):
    chunk = x.shape if same else x.shape[1:]
    return pl.pallas_call(
        functools.partial(exchange_kernel, axis, other_axis, n, same),
        out_shape=jax.ShapeDtypeStruct((n,) + chunk, x.dtype),
        in_specs=[pl.BlockSpec(memory_space=pltpu.VMEM)],
        out_specs=pl.BlockSpec(memory_space=pltpu.VMEM),
        scratch_shapes=[
            pltpu.VMEM((n,) + chunk, x.dtype),
            pltpu.SemaphoreType.DMA((n,)),
            pltpu.SemaphoreType.DMA((n,)),
        ],
        compiler_params=pltpu.CompilerParams(
            collective_id=collective_id, has_side_effects=True
        ),
    )(x)


def per_device(kernel, slip_delta, block_list, live_count, direct_effect, load_rate, time_before):
    nrows = lax.axis_size("rows")
    ncols = lax.axis_size("cols")
    my_row = lax.axis_index("rows")
    events_here, list_here, _ = slip_delta.shape
    blocks = kernel.shape[1] // BLOCK
    entry = my_row * list_here + jnp.arange(list_here, dtype=jnp.int32)
    live = entry[None, :] < live_count[:, None]
    key = jnp.where(live, block_list, -1).astype(jnp.float32)
    payload = jnp.stack(
        [slip_delta, jnp.broadcast_to(key[:, :, None], slip_delta.shape)], axis=0
    )
    gathered = exchange(payload, "rows", "cols", nrows, True, 1)
    gathered = jnp.moveaxis(gathered, 0, 2).reshape(2, events_here, nrows * list_here, BLOCK)
    slip_full = gathered[0]
    key_full = gathered[1][:, :, 0].astype(jnp.int32)
    total_blocks = blocks * ncols
    onehot = (
        key_full[:, :, None] == jnp.arange(total_blocks, dtype=jnp.int32)[None, None, :]
    ).astype(jnp.float32)
    dense_own = jnp.einsum("ebj,ebc->ejc", onehot, slip_full, precision=lax.Precision.HIGHEST)
    dense_own = dense_own.reshape(events_here, ncols, blocks * BLOCK)
    dense_own = jnp.moveaxis(dense_own, 1, 0)
    stress_change = stress_sum(kernel, dense_own, ncols)
    scale = direct_effect[:, None]
    growth = jnp.expm1(load_rate * time_before / direct_effect)[:, None]
    log_time = jnp.log(scale / load_rate[:, None]) + jnp.log(
        jnp.log1p(jnp.exp(-stress_change / scale) * growth)
    )
    return (stress_change, log_time)


def solution(mesh):
    in_specs = (
        P("rows", "cols"),
        P("cols", "rows", None),
        P("cols", "rows"),
        P("cols"),
        P(("rows", "cols")),
        P(("rows", "cols")),
        P(("rows", "cols")),
    )
    out_specs = (P(("rows", "cols"), None), P(("rows", "cols"), None))
    return jax.shard_map(
        per_device, mesh=mesh, in_specs=in_specs, out_specs=out_specs, check_vma=False
    )
```

```python
import functools

import jax
import jax.numpy as jnp
from jax import lax
from jax.experimental import pallas as pl
from jax.experimental.pallas import tpu as pltpu
from jax.sharding import PartitionSpec as P

BLOCK = 128
MESH = pl.DeviceIdType.MESH


def stress_kernel(ncols, groups, own_ref, kernel_hbm, out_ref, kmat, dense, sendbuf, slots, kload_sem, local_sem, a_send, a_recv, send_sem, recv_sem):
    me = lax.axis_index("cols")
    row = lax.axis_index("rows")
    share = out_ref.shape[0]
    per_group = ncols // groups
    here = own_ref.shape[1]
    quarter = kmat.shape[0] // 4

    loads = []
    for q in range(4):
        load = pltpu.make_async_copy(
            kernel_hbm.at[pl.ds(q * quarter, quarter)], kmat.at[pl.ds(q * quarter, quarter)], kload_sem.at[q]
        )
        load.start()
        loads.append(load)

    barrier = pltpu.get_barrier_semaphore()
    for k in range(1, ncols):
        peer = lax.rem(me + k, ncols)
        pl.semaphore_signal(barrier, inc=1, device_id=(row, peer), device_id_type=MESH)
    pl.semaphore_wait(barrier, ncols - 1)

    sends = []
    for k in range(1, ncols):
        peer = lax.rem(me + k, ncols)
        copy = pltpu.make_async_remote_copy(
            src_ref=own_ref.at[peer],
            dst_ref=dense.at[pl.ds(me * here, here)],
            send_sem=a_send.at[peer],
            recv_sem=a_recv.at[me],
            device_id=(row, peer),
            device_id_type=MESH,
        )
        copy.start()
        sends.append(copy)
    local = pltpu.make_async_copy(own_ref.at[me], dense.at[pl.ds(me * here, here)], local_sem)
    local.start()
    local.wait()
    for k in range(1, ncols):
        src = lax.rem(me + ncols - k, ncols)
        pltpu.make_async_remote_copy(
            src_ref=own_ref.at[src],
            dst_ref=dense.at[pl.ds(src * here, here)],
            send_sem=a_send.at[src],
            recv_sem=a_recv.at[src],
            device_id=(row, src),
            device_id_type=MESH,
        ).wait_recv()
    for load in loads:
        load.wait()

    rs_sends = []
    for g in range(groups):
        rows = pl.ds(g * per_group * share, per_group * share)
        part = lax.dot_general(
            kmat[rows, :],
            dense[...],
            (((1,), (1,)), ((), ())),
            precision=lax.Precision.HIGHEST,
            preferred_element_type=jnp.float32,
        )
        for j in range(per_group):
            dest = g * per_group + j
            sendbuf[dest] = part[j * share:(j + 1) * share]
            copy = pltpu.make_async_remote_copy(
                src_ref=sendbuf.at[dest],
                dst_ref=slots.at[me],
                send_sem=send_sem.at[dest],
                recv_sem=recv_sem.at[me],
                device_id=(row, dest),
                device_id_type=MESH,
            )

            @pl.when(me != dest)
            def _():
                copy.start()

            rs_sends.append((dest, copy))

    total = sendbuf[me]
    for k in range(1, ncols):
        src = lax.rem(me + ncols - k, ncols)
        pltpu.make_async_remote_copy(
            src_ref=sendbuf.at[src],
            dst_ref=slots.at[src],
            send_sem=send_sem.at[src],
            recv_sem=recv_sem.at[src],
            device_id=(row, src),
            device_id_type=MESH,
        ).wait_recv()
        total = total + slots[src]
    out_ref[...] = total
    for copy in sends:
        copy.wait_send()
    for dest, copy in rs_sends:

        @pl.when(me != dest)
        def _():
            copy.wait_send()


def stress_sum(kernel, dense_own, ncols, groups=4):
    rows, sources = kernel.shape
    here = dense_own.shape[1]
    events = ncols * here
    share = rows // ncols
    return pl.pallas_call(
        functools.partial(stress_kernel, ncols, groups),
        out_shape=jax.ShapeDtypeStruct((share, events), jnp.float32),
        in_specs=[pl.BlockSpec(memory_space=pltpu.VMEM), pl.BlockSpec(memory_space=pl.ANY)],
        out_specs=pl.BlockSpec(memory_space=pltpu.VMEM),
        scratch_shapes=[
            pltpu.VMEM((rows, sources), jnp.float32),
            pltpu.VMEM((events, sources), jnp.float32),
            pltpu.VMEM((ncols, share, events), jnp.float32),
            pltpu.VMEM((ncols, share, events), jnp.float32),
            pltpu.SemaphoreType.DMA((4,)),
            pltpu.SemaphoreType.DMA,
            pltpu.SemaphoreType.DMA((ncols,)),
            pltpu.SemaphoreType.DMA((ncols,)),
            pltpu.SemaphoreType.DMA((ncols,)),
            pltpu.SemaphoreType.DMA((ncols,)),
        ],
        compiler_params=pltpu.CompilerParams(
            collective_id=0, has_side_effects=True
        ),
    )(dense_own, kernel)


def exchange_kernel(axis, other_axis, n, same, x_ref, out_ref, slots, send_sem, recv_sem):
    me = lax.axis_index(axis)
    other = lax.axis_index(other_axis)

    def device(peer):
        return (other, peer) if axis == "cols" else (peer, other)

    barrier = pltpu.get_barrier_semaphore()
    for k in range(1, n):
        peer = lax.rem(me + k, n)
        pl.semaphore_signal(barrier, inc=1, device_id=device(peer), device_id_type=MESH)
    pl.semaphore_wait(barrier, n - 1)

    copies = []
    for k in range(1, n):
        peer = lax.rem(me + k, n)
        copy = pltpu.make_async_remote_copy(
            src_ref=x_ref if same else x_ref.at[peer],
            dst_ref=slots.at[me],
            send_sem=send_sem.at[peer],
            recv_sem=recv_sem.at[me],
            device_id=device(peer),
            device_id_type=MESH,
        )
        copy.start()
        copies.append(copy)

    out_ref[me] = x_ref[...] if same else x_ref[me]
    for k in range(1, n):
        src = lax.rem(me + n - k, n)
        pltpu.make_async_remote_copy(
            src_ref=x_ref if same else x_ref.at[src],
            dst_ref=slots.at[src],
            send_sem=send_sem.at[src],
            recv_sem=recv_sem.at[src],
            device_id=device(src),
            device_id_type=MESH,
        ).wait_recv()
        out_ref[src] = slots[src]
    for copy in copies:
        copy.wait_send()


def exchange(x, axis, other_axis, n, same, collective_id):
    chunk = x.shape if same else x.shape[1:]
    return pl.pallas_call(
        functools.partial(exchange_kernel, axis, other_axis, n, same),
        out_shape=jax.ShapeDtypeStruct((n,) + chunk, x.dtype),
        in_specs=[pl.BlockSpec(memory_space=pltpu.VMEM)],
        out_specs=pl.BlockSpec(memory_space=pltpu.VMEM),
        scratch_shapes=[
            pltpu.VMEM((n,) + chunk, x.dtype),
            pltpu.SemaphoreType.DMA((n,)),
            pltpu.SemaphoreType.DMA((n,)),
        ],
        compiler_params=pltpu.CompilerParams(
            collective_id=collective_id, has_side_effects=True
        ),
    )(x)


def per_device(kernel, slip_delta, block_list, live_count, direct_effect, load_rate, time_before):
    nrows = lax.axis_size("rows")
    ncols = lax.axis_size("cols")
    my_row = lax.axis_index("rows")
    events_here, list_here, _ = slip_delta.shape
    blocks = kernel.shape[1] // BLOCK
    entry = my_row * list_here + jnp.arange(list_here, dtype=jnp.int32)
    live = entry[None, :] < live_count[:, None]
    key = jnp.where(live, block_list, -1).astype(jnp.float32)
    payload = jnp.stack(
        [slip_delta, jnp.broadcast_to(key[:, :, None], slip_delta.shape)], axis=0
    )
    gathered = exchange(payload, "rows", "cols", nrows, True, 1)
    gathered = jnp.moveaxis(gathered, 0, 2).reshape(2, events_here, nrows * list_here, BLOCK)
    slip_full = gathered[0]
    key_full = gathered[1][:, :, 0].astype(jnp.int32)
    total_blocks = blocks * ncols
    onehot = (
        key_full[:, :, None] == jnp.arange(total_blocks, dtype=jnp.int32)[None, None, :]
    ).astype(jnp.float32)
    dense_own = jnp.einsum("ebj,ebc->ejc", onehot, slip_full, precision=lax.Precision.HIGHEST)
    dense_own = dense_own.reshape(events_here, ncols, blocks * BLOCK)
    dense_own = jnp.moveaxis(dense_own, 1, 0)
    stress_change = stress_sum(kernel, dense_own, ncols)
    scale = direct_effect[:, None]
    growth = jnp.expm1(load_rate * time_before / direct_effect)[:, None]
    log_time = jnp.log(scale / load_rate[:, None]) + jnp.log(
        jnp.log1p(jnp.exp(-stress_change / scale) * growth)
    )
    return (stress_change, log_time)


def solution(mesh):
    in_specs = (
        P("rows", "cols"),
        P("cols", "rows", None),
        P("cols", "rows"),
        P("cols"),
        P(("rows", "cols")),
        P(("rows", "cols")),
        P(("rows", "cols")),
    )
    out_specs = (P(("rows", "cols"), None), P(("rows", "cols"), None))
    return jax.shard_map(
        per_device, mesh=mesh, in_specs=in_specs, out_specs=out_specs, check_vma=False
    )
```

```python
import functools

import jax
import jax.numpy as jnp
from jax import lax
from jax.experimental import pallas as pl
from jax.experimental.pallas import tpu as pltpu
from jax.sharding import PartitionSpec as P

BLOCK = 128
MESH = pl.DeviceIdType.MESH


def stress_kernel(ncols, groups, own_ref, kernel_hbm, out_ref, kmat, dense, sendbuf, slots, kload_sem, local_sem, a_send, a_recv, send_sem, recv_sem):
    me = lax.axis_index("cols")
    row = lax.axis_index("rows")
    share = out_ref.shape[0]
    per_group = ncols // groups
    here = own_ref.shape[1]
    quarter = kmat.shape[0] // 4

    loads = []
    for q in range(4):
        load = pltpu.make_async_copy(
            kernel_hbm.at[pl.ds(q * quarter, quarter)], kmat.at[pl.ds(q * quarter, quarter)], kload_sem.at[q]
        )
        load.start()
        loads.append(load)

    barrier = pltpu.get_barrier_semaphore()
    for k in range(1, ncols):
        peer = lax.rem(me + k, ncols)
        pl.semaphore_signal(barrier, inc=1, device_id=(row, peer), device_id_type=MESH)
    pl.semaphore_wait(barrier, ncols - 1)

    sends = []
    for k in range(1, ncols):
        peer = lax.rem(me + k, ncols)
        copy = pltpu.make_async_remote_copy(
            src_ref=own_ref.at[peer],
            dst_ref=dense.at[pl.ds(me * here, here)],
            send_sem=a_send.at[peer],
            recv_sem=a_recv.at[me],
            device_id=(row, peer),
            device_id_type=MESH,
        )
        copy.start()
        sends.append(copy)
    local = pltpu.make_async_copy(own_ref.at[me], dense.at[pl.ds(me * here, here)], local_sem)
    local.start()
    local.wait()
    for k in range(1, ncols):
        src = lax.rem(me + ncols - k, ncols)
        pltpu.make_async_remote_copy(
            src_ref=own_ref.at[src],
            dst_ref=dense.at[pl.ds(src * here, here)],
            send_sem=a_send.at[src],
            recv_sem=a_recv.at[src],
            device_id=(row, src),
            device_id_type=MESH,
        ).wait_recv()
    for load in loads:
        load.wait()

    rs_sends = []
    for g in range(groups):
        rows = pl.ds(g * per_group * share, per_group * share)
        part = lax.dot_general(
            kmat[rows, :],
            dense[...],
            (((1,), (1,)), ((), ())),
            precision=lax.Precision.HIGH,
            preferred_element_type=jnp.float32,
        )
        for j in range(per_group):
            dest = g * per_group + j
            sendbuf[dest] = part[j * share:(j + 1) * share]
            copy = pltpu.make_async_remote_copy(
                src_ref=sendbuf.at[dest],
                dst_ref=slots.at[me],
                send_sem=send_sem.at[dest],
                recv_sem=recv_sem.at[me],
                device_id=(row, dest),
                device_id_type=MESH,
            )

            @pl.when(me != dest)
            def _():
                copy.start()

            rs_sends.append((dest, copy))

    total = sendbuf[me]
    for k in range(1, ncols):
        src = lax.rem(me + ncols - k, ncols)
        pltpu.make_async_remote_copy(
            src_ref=sendbuf.at[src],
            dst_ref=slots.at[src],
            send_sem=send_sem.at[src],
            recv_sem=recv_sem.at[src],
            device_id=(row, src),
            device_id_type=MESH,
        ).wait_recv()
        total = total + slots[src]
    out_ref[...] = total
    for copy in sends:
        copy.wait_send()
    for dest, copy in rs_sends:

        @pl.when(me != dest)
        def _():
            copy.wait_send()


def stress_sum(kernel, dense_own, ncols, groups=4):
    rows, sources = kernel.shape
    here = dense_own.shape[1]
    events = ncols * here
    share = rows // ncols
    return pl.pallas_call(
        functools.partial(stress_kernel, ncols, groups),
        out_shape=jax.ShapeDtypeStruct((share, events), jnp.float32),
        in_specs=[pl.BlockSpec(memory_space=pltpu.VMEM), pl.BlockSpec(memory_space=pl.ANY)],
        out_specs=pl.BlockSpec(memory_space=pltpu.VMEM),
        scratch_shapes=[
            pltpu.VMEM((rows, sources), jnp.float32),
            pltpu.VMEM((events, sources), jnp.float32),
            pltpu.VMEM((ncols, share, events), jnp.float32),
            pltpu.VMEM((ncols, share, events), jnp.float32),
            pltpu.SemaphoreType.DMA((4,)),
            pltpu.SemaphoreType.DMA,
            pltpu.SemaphoreType.DMA((ncols,)),
            pltpu.SemaphoreType.DMA((ncols,)),
            pltpu.SemaphoreType.DMA((ncols,)),
            pltpu.SemaphoreType.DMA((ncols,)),
        ],
        compiler_params=pltpu.CompilerParams(
            collective_id=0, has_side_effects=True
        ),
    )(dense_own, kernel)


def exchange_kernel(axis, other_axis, n, same, x_ref, out_ref, slots, send_sem, recv_sem):
    me = lax.axis_index(axis)
    other = lax.axis_index(other_axis)

    def device(peer):
        return (other, peer) if axis == "cols" else (peer, other)

    barrier = pltpu.get_barrier_semaphore()
    for k in range(1, n):
        peer = lax.rem(me + k, n)
        pl.semaphore_signal(barrier, inc=1, device_id=device(peer), device_id_type=MESH)
    pl.semaphore_wait(barrier, n - 1)

    copies = []
    for k in range(1, n):
        peer = lax.rem(me + k, n)
        copy = pltpu.make_async_remote_copy(
            src_ref=x_ref if same else x_ref.at[peer],
            dst_ref=slots.at[me],
            send_sem=send_sem.at[peer],
            recv_sem=recv_sem.at[me],
            device_id=device(peer),
            device_id_type=MESH,
        )
        copy.start()
        copies.append(copy)

    out_ref[me] = x_ref[...] if same else x_ref[me]
    for k in range(1, n):
        src = lax.rem(me + n - k, n)
        pltpu.make_async_remote_copy(
            src_ref=x_ref if same else x_ref.at[src],
            dst_ref=slots.at[src],
            send_sem=send_sem.at[src],
            recv_sem=recv_sem.at[src],
            device_id=device(src),
            device_id_type=MESH,
        ).wait_recv()
        out_ref[src] = slots[src]
    for copy in copies:
        copy.wait_send()


def exchange(x, axis, other_axis, n, same, collective_id):
    chunk = x.shape if same else x.shape[1:]
    return pl.pallas_call(
        functools.partial(exchange_kernel, axis, other_axis, n, same),
        out_shape=jax.ShapeDtypeStruct((n,) + chunk, x.dtype),
        in_specs=[pl.BlockSpec(memory_space=pltpu.VMEM)],
        out_specs=pl.BlockSpec(memory_space=pltpu.VMEM),
        scratch_shapes=[
            pltpu.VMEM((n,) + chunk, x.dtype),
            pltpu.SemaphoreType.DMA((n,)),
            pltpu.SemaphoreType.DMA((n,)),
        ],
        compiler_params=pltpu.CompilerParams(
            collective_id=collective_id, has_side_effects=True
        ),
    )(x)


def per_device(kernel, slip_delta, block_list, live_count, direct_effect, load_rate, time_before):
    nrows = lax.axis_size("rows")
    ncols = lax.axis_size("cols")
    my_row = lax.axis_index("rows")
    events_here, list_here, _ = slip_delta.shape
    blocks = kernel.shape[1] // BLOCK
    entry = my_row * list_here + jnp.arange(list_here, dtype=jnp.int32)
    live = entry[None, :] < live_count[:, None]
    key = jnp.where(live, block_list, -1).astype(jnp.float32)
    payload = jnp.stack(
        [slip_delta, jnp.broadcast_to(key[:, :, None], slip_delta.shape)], axis=0
    )
    gathered = exchange(payload, "rows", "cols", nrows, True, 1)
    gathered = jnp.moveaxis(gathered, 0, 2).reshape(2, events_here, nrows * list_here, BLOCK)
    slip_full = gathered[0]
    key_full = gathered[1][:, :, 0].astype(jnp.int32)
    total_blocks = blocks * ncols
    onehot = (
        key_full[:, :, None] == jnp.arange(total_blocks, dtype=jnp.int32)[None, None, :]
    ).astype(jnp.float32)
    dense_own = jnp.einsum("ebj,ebc->ejc", onehot, slip_full, precision=lax.Precision.HIGHEST)
    dense_own = dense_own.reshape(events_here, ncols, blocks * BLOCK)
    dense_own = jnp.moveaxis(dense_own, 1, 0)
    stress_change = stress_sum(kernel, dense_own, ncols)
    scale = direct_effect[:, None]
    growth = jnp.expm1(load_rate * time_before / direct_effect)[:, None]
    log_time = jnp.log(scale / load_rate[:, None]) + jnp.log(
        jnp.log1p(jnp.exp(-stress_change / scale) * growth)
    )
    return (stress_change, log_time)


def solution(mesh):
    in_specs = (
        P("rows", "cols"),
        P("cols", "rows", None),
        P("cols", "rows"),
        P("cols"),
        P(("rows", "cols")),
        P(("rows", "cols")),
        P(("rows", "cols")),
    )
    out_specs = (P(("rows", "cols"), None), P(("rows", "cols"), None))
    return jax.shard_map(
        per_device, mesh=mesh, in_specs=in_specs, out_specs=out_specs, check_vma=False
    )
```

```python
import functools

import jax
import jax.numpy as jnp
from jax import lax
from jax.experimental import pallas as pl
from jax.experimental.pallas import tpu as pltpu
from jax.sharding import PartitionSpec as P

BLOCK = 128
MESH = pl.DeviceIdType.MESH


def stress_kernel(nrows, ncols, groups, pay_ref, kernel_hbm, out_ref, kmat, gathered, dense_own, landed, dense, sendbuf, slots,
                  kload_sem, local_sem, g_send, g_recv, a_send, a_recv, r_send, r_recv, send_sem, recv_sem):
    me = lax.axis_index("cols")
    my_row = lax.axis_index("rows")
    share = out_ref.shape[0]
    per_group = ncols // groups
    _, here, list_here, patch = pay_ref.shape
    blocks = kmat.shape[1] // patch
    quarter = kmat.shape[0] // 4

    loads = []
    for q in range(4):
        load = pltpu.make_async_copy(
            kernel_hbm.at[pl.ds(q * quarter, quarter)], kmat.at[pl.ds(q * quarter, quarter)], kload_sem.at[q]
        )
        load.start()
        loads.append(load)

    barrier = pltpu.get_barrier_semaphore()
    for k in range(1, nrows):
        peer = lax.rem(my_row + k, nrows)
        pl.semaphore_signal(barrier, inc=1, device_id=(peer, me), device_id_type=MESH)
    for k in range(1, ncols):
        peer = lax.rem(me + k, ncols)
        pl.semaphore_signal(barrier, inc=1, device_id=(my_row, peer), device_id_type=MESH)
    pl.semaphore_wait(barrier, nrows + ncols - 2)

    def entries(r):
        return pl.ds(pl.multiple_of(r * list_here, list_here), list_here)

    sends = []
    for k in range(1, nrows):
        peer = lax.rem(my_row + k, nrows)
        copy = pltpu.make_async_remote_copy(
            src_ref=pay_ref,
            dst_ref=gathered.at[:, :, entries(my_row)],
            send_sem=g_send.at[peer],
            recv_sem=g_recv.at[my_row],
            device_id=(peer, me),
            device_id_type=MESH,
        )
        copy.start()
        sends.append(copy)
    local = pltpu.make_async_copy(pay_ref, gathered.at[:, :, entries(my_row)], local_sem)
    local.start()
    local.wait()
    for k in range(1, nrows):
        src = lax.rem(my_row + nrows - k, nrows)
        pltpu.make_async_remote_copy(
            src_ref=pay_ref,
            dst_ref=gathered.at[:, :, entries(src)],
            send_sem=g_send.at[src],
            recv_sem=g_recv.at[src],
            device_id=(src, me),
            device_id_type=MESH,
        ).wait_recv()

    total_blocks = dense_own.shape[1]
    lane = lax.broadcasted_iota(jnp.int32, (nrows * list_here, patch), 1)
    for e in range(here):
        keys = gathered[1, e].astype(jnp.int32)
        slip = gathered[0, e]
        for q in range(total_blocks // patch):
            onehot = (keys == lane + q * patch).astype(jnp.float32)
            dense_own[e, pl.ds(q * patch, patch), :] = lax.dot_general(
                onehot,
                slip,
                (((0,), (0,)), ((), ())),
                precision=lax.Precision.HIGHEST,
                preferred_element_type=jnp.float32,
            )

    def mine(c):
        return pl.ds(pl.multiple_of(c * blocks, blocks), blocks)

    def slot(c):
        return pl.ds(pl.multiple_of(c * here, here), here)

    for k in range(1, ncols):
        peer = lax.rem(me + k, ncols)
        copy = pltpu.make_async_remote_copy(
            src_ref=dense_own.at[:, mine(peer)],
            dst_ref=landed.at[slot(me)],
            send_sem=a_send.at[peer],
            recv_sem=a_recv.at[me],
            device_id=(my_row, peer),
            device_id_type=MESH,
        )
        copy.start()
        sends.append(copy)
    local = pltpu.make_async_copy(dense_own.at[:, mine(me)], landed.at[slot(me)], local_sem)
    local.start()
    local.wait()
    for k in range(1, ncols):
        src = lax.rem(me + ncols - k, ncols)
        pltpu.make_async_remote_copy(
            src_ref=dense_own.at[:, mine(src)],
            dst_ref=landed.at[slot(src)],
            send_sem=a_send.at[src],
            recv_sem=a_recv.at[src],
            device_id=(my_row, src),
            device_id_type=MESH,
        ).wait_recv()

    relayout = []
    for j in range(blocks):
        copy = pltpu.make_async_copy(landed.at[:, j], dense.at[j], r_send.at[j])
        copy.start()
        relayout.append(copy)
    for copy in relayout:
        copy.wait()
    for load in loads:
        load.wait()

    rs_sends = []
    for g in range(groups):
        rows = pl.ds(g * per_group * share, per_group * share)
        part = None
        for j in range(blocks):
            term = lax.dot_general(
                kmat[rows, pl.ds(j * patch, patch)],
                dense[j],
                (((1,), (1,)), ((), ())),
                precision=lax.Precision.HIGH,
                preferred_element_type=jnp.float32,
            )
            part = term if part is None else part + term
        for j in range(per_group):
            dest = g * per_group + j
            sendbuf[dest] = part[j * share:(j + 1) * share]
            copy = pltpu.make_async_remote_copy(
                src_ref=sendbuf.at[dest],
                dst_ref=slots.at[me],
                send_sem=send_sem.at[dest],
                recv_sem=recv_sem.at[me],
                device_id=(my_row, dest),
                device_id_type=MESH,
            )

            @pl.when(me != dest)
            def _():
                copy.start()

            rs_sends.append((dest, copy))

    total = sendbuf[me]
    for k in range(1, ncols):
        src = lax.rem(me + ncols - k, ncols)
        pltpu.make_async_remote_copy(
            src_ref=sendbuf.at[src],
            dst_ref=slots.at[src],
            send_sem=send_sem.at[src],
            recv_sem=recv_sem.at[src],
            device_id=(my_row, src),
            device_id_type=MESH,
        ).wait_recv()
        total = total + slots[src]
    out_ref[...] = total
    for copy in sends:
        copy.wait_send()
    for dest, copy in rs_sends:

        @pl.when(me != dest)
        def _():
            copy.wait_send()


def stress_sum(kernel, payload, nrows, ncols, groups=4):
    rows, sources = kernel.shape
    _, here, list_here, patch = payload.shape
    events = ncols * here
    share = rows // ncols
    blocks = sources // patch
    return pl.pallas_call(
        functools.partial(stress_kernel, nrows, ncols, groups),
        out_shape=jax.ShapeDtypeStruct((share, events), jnp.float32),
        in_specs=[pl.BlockSpec(memory_space=pltpu.VMEM), pl.BlockSpec(memory_space=pl.ANY)],
        out_specs=pl.BlockSpec(memory_space=pltpu.VMEM),
        scratch_shapes=[
            pltpu.VMEM((rows, sources), jnp.float32),
            pltpu.VMEM((2, here, nrows * list_here, patch), jnp.float32),
            pltpu.VMEM((here, ncols * blocks, patch), jnp.float32),
            pltpu.VMEM((events, blocks, patch), jnp.float32),
            pltpu.VMEM((blocks, events, patch), jnp.float32),
            pltpu.VMEM((ncols, share, events), jnp.float32),
            pltpu.VMEM((ncols, share, events), jnp.float32),
            pltpu.SemaphoreType.DMA((4,)),
            pltpu.SemaphoreType.DMA,
            pltpu.SemaphoreType.DMA((nrows,)),
            pltpu.SemaphoreType.DMA((nrows,)),
            pltpu.SemaphoreType.DMA((ncols,)),
            pltpu.SemaphoreType.DMA((ncols,)),
            pltpu.SemaphoreType.DMA((blocks,)),
            pltpu.SemaphoreType.DMA((blocks,)),
            pltpu.SemaphoreType.DMA((ncols,)),
            pltpu.SemaphoreType.DMA((ncols,)),
        ],
        compiler_params=pltpu.CompilerParams(collective_id=0, has_side_effects=True),
    )(payload, kernel)


def per_device(kernel, slip_delta, block_list, live_count, direct_effect, load_rate, time_before):
    nrows = lax.axis_size("rows")
    ncols = lax.axis_size("cols")
    my_row = lax.axis_index("rows")
    list_here = slip_delta.shape[1]
    entry = my_row * list_here + jnp.arange(list_here, dtype=jnp.int32)
    live = entry[None, :] < live_count[:, None]
    key = jnp.where(live, block_list, -1).astype(jnp.float32)
    payload = jnp.stack(
        [slip_delta, jnp.broadcast_to(key[:, :, None], slip_delta.shape)], axis=0
    )
    stress_change = stress_sum(kernel, payload, nrows, ncols)
    scale = direct_effect[:, None]
    growth = jnp.expm1(load_rate * time_before / direct_effect)[:, None]
    log_time = jnp.log(scale / load_rate[:, None]) + jnp.log(
        jnp.log1p(jnp.exp(-stress_change / scale) * growth)
    )
    return (stress_change, log_time)


def solution(mesh):
    in_specs = (
        P("rows", "cols"),
        P("cols", "rows", None),
        P("cols", "rows"),
        P("cols"),
        P(("rows", "cols")),
        P(("rows", "cols")),
        P(("rows", "cols")),
    )
    out_specs = (P(("rows", "cols"), None), P(("rows", "cols"), None))
    return jax.shard_map(
        per_device, mesh=mesh, in_specs=in_specs, out_specs=out_specs, check_vma=False
    )
```

```python
import functools

import jax
import jax.numpy as jnp
from jax import lax
from jax.experimental import pallas as pl
from jax.experimental.pallas import tpu as pltpu
from jax.sharding import PartitionSpec as P

BLOCK = 128
MESH = pl.DeviceIdType.MESH


def stress_kernel(nrows, ncols, groups, slip_ref, list_ref, count_ref, kernel_hbm, out_ref, pay_ref, kmat, gathered, dense_own,
                  landed, dense, sendbuf, slots, kload_sem, local_sem, g_send, g_recv, a_send, a_recv, r_send, r_recv, send_sem, recv_sem):
    me = lax.axis_index("cols")
    my_row = lax.axis_index("rows")
    share = out_ref.shape[0]
    per_group = ncols // groups
    here, list_here, patch = slip_ref.shape
    blocks = kmat.shape[1] // patch
    quarter = kmat.shape[0] // 4

    loads = []
    for q in range(4):
        load = pltpu.make_async_copy(
            kernel_hbm.at[pl.ds(q * quarter, quarter)], kmat.at[pl.ds(q * quarter, quarter)], kload_sem.at[q]
        )
        load.start()
        loads.append(load)

    pay_ref[0] = slip_ref[...]
    for e in range(here):
        for b in range(list_here):
            live = my_row * list_here + b < count_ref[e]
            key = jnp.where(live, list_ref[e, b], -1)
            pay_ref[1, e, pl.ds(b, 1), :] = jnp.full((1, patch), key, jnp.int32).astype(jnp.float32)

    barrier = pltpu.get_barrier_semaphore()
    for k in range(1, nrows):
        peer = lax.rem(my_row + k, nrows)
        pl.semaphore_signal(barrier, inc=1, device_id=(peer, me), device_id_type=MESH)
    for k in range(1, ncols):
        peer = lax.rem(me + k, ncols)
        pl.semaphore_signal(barrier, inc=1, device_id=(my_row, peer), device_id_type=MESH)
    pl.semaphore_wait(barrier, nrows + ncols - 2)

    def entries(r):
        return pl.ds(pl.multiple_of(r * list_here, list_here), list_here)

    sends = []
    for k in range(1, nrows):
        peer = lax.rem(my_row + k, nrows)
        copy = pltpu.make_async_remote_copy(
            src_ref=pay_ref,
            dst_ref=gathered.at[:, :, entries(my_row)],
            send_sem=g_send.at[peer],
            recv_sem=g_recv.at[my_row],
            device_id=(peer, me),
            device_id_type=MESH,
        )
        copy.start()
        sends.append(copy)
    local = pltpu.make_async_copy(pay_ref, gathered.at[:, :, entries(my_row)], local_sem)
    local.start()
    local.wait()
    for k in range(1, nrows):
        src = lax.rem(my_row + nrows - k, nrows)
        pltpu.make_async_remote_copy(
            src_ref=pay_ref,
            dst_ref=gathered.at[:, :, entries(src)],
            send_sem=g_send.at[src],
            recv_sem=g_recv.at[src],
            device_id=(src, me),
            device_id_type=MESH,
        ).wait_recv()

    total_blocks = dense_own.shape[1]
    lane = lax.broadcasted_iota(jnp.int32, (nrows * list_here, patch), 1)
    for e in range(here):
        keys = gathered[1, e].astype(jnp.int32)
        slip = gathered[0, e]
        for q in range(total_blocks // patch):
            onehot = (keys == lane + q * patch).astype(jnp.float32)
            dense_own[e, pl.ds(q * patch, patch), :] = lax.dot_general(
                onehot,
                slip,
                (((0,), (0,)), ((), ())),
                precision=lax.Precision.HIGHEST,
                preferred_element_type=jnp.float32,
            )

    def mine(c):
        return pl.ds(pl.multiple_of(c * blocks, blocks), blocks)

    def slot(c):
        return pl.ds(pl.multiple_of(c * here, here), here)

    for k in range(1, ncols):
        peer = lax.rem(me + k, ncols)
        copy = pltpu.make_async_remote_copy(
            src_ref=dense_own.at[:, mine(peer)],
            dst_ref=landed.at[slot(me)],
            send_sem=a_send.at[peer],
            recv_sem=a_recv.at[me],
            device_id=(my_row, peer),
            device_id_type=MESH,
        )
        copy.start()
        sends.append(copy)
    local = pltpu.make_async_copy(dense_own.at[:, mine(me)], landed.at[slot(me)], local_sem)
    local.start()
    local.wait()
    for k in range(1, ncols):
        src = lax.rem(me + ncols - k, ncols)
        pltpu.make_async_remote_copy(
            src_ref=dense_own.at[:, mine(src)],
            dst_ref=landed.at[slot(src)],
            send_sem=a_send.at[src],
            recv_sem=a_recv.at[src],
            device_id=(my_row, src),
            device_id_type=MESH,
        ).wait_recv()

    relayout = []
    for j in range(blocks):
        copy = pltpu.make_async_copy(landed.at[:, j], dense.at[j], r_send.at[j])
        copy.start()
        relayout.append(copy)
    for copy in relayout:
        copy.wait()
    for load in loads:
        load.wait()

    rs_sends = []
    for g in range(groups):
        rows = pl.ds(g * per_group * share, per_group * share)
        part = None
        for j in range(blocks):
            term = lax.dot_general(
                kmat[rows, pl.ds(j * patch, patch)],
                dense[j],
                (((1,), (1,)), ((), ())),
                precision=lax.Precision.HIGH,
                preferred_element_type=jnp.float32,
            )
            part = term if part is None else part + term
        for j in range(per_group):
            dest = g * per_group + j
            sendbuf[dest] = part[j * share:(j + 1) * share]
            copy = pltpu.make_async_remote_copy(
                src_ref=sendbuf.at[dest],
                dst_ref=slots.at[me],
                send_sem=send_sem.at[dest],
                recv_sem=recv_sem.at[me],
                device_id=(my_row, dest),
                device_id_type=MESH,
            )

            @pl.when(me != dest)
            def _():
                copy.start()

            rs_sends.append((dest, copy))

    total = sendbuf[me]
    for k in range(1, ncols):
        src = lax.rem(me + ncols - k, ncols)
        pltpu.make_async_remote_copy(
            src_ref=sendbuf.at[src],
            dst_ref=slots.at[src],
            send_sem=send_sem.at[src],
            recv_sem=recv_sem.at[src],
            device_id=(my_row, src),
            device_id_type=MESH,
        ).wait_recv()
        total = total + slots[src]
    out_ref[...] = total
    for copy in sends:
        copy.wait_send()
    for dest, copy in rs_sends:

        @pl.when(me != dest)
        def _():
            copy.wait_send()


def stress_sum(kernel, slip_delta, block_list, live_count, nrows, ncols, groups=4):
    rows, sources = kernel.shape
    here, list_here, patch = slip_delta.shape
    events = ncols * here
    share = rows // ncols
    blocks = sources // patch
    return pl.pallas_call(
        functools.partial(stress_kernel, nrows, ncols, groups),
        out_shape=jax.ShapeDtypeStruct((share, events), jnp.float32),
        in_specs=[
            pl.BlockSpec(memory_space=pltpu.VMEM),
            pl.BlockSpec(memory_space=pltpu.SMEM),
            pl.BlockSpec(memory_space=pltpu.SMEM),
            pl.BlockSpec(memory_space=pl.ANY),
        ],
        out_specs=pl.BlockSpec(memory_space=pltpu.VMEM),
        scratch_shapes=[
            pltpu.VMEM((2, here, list_here, patch), jnp.float32),
            pltpu.VMEM((rows, sources), jnp.float32),
            pltpu.VMEM((2, here, nrows * list_here, patch), jnp.float32),
            pltpu.VMEM((here, ncols * blocks, patch), jnp.float32),
            pltpu.VMEM((events, blocks, patch), jnp.float32),
            pltpu.VMEM((blocks, events, patch), jnp.float32),
            pltpu.VMEM((ncols, share, events), jnp.float32),
            pltpu.VMEM((ncols, share, events), jnp.float32),
            pltpu.SemaphoreType.DMA((4,)),
            pltpu.SemaphoreType.DMA,
            pltpu.SemaphoreType.DMA((nrows,)),
            pltpu.SemaphoreType.DMA((nrows,)),
            pltpu.SemaphoreType.DMA((ncols,)),
            pltpu.SemaphoreType.DMA((ncols,)),
            pltpu.SemaphoreType.DMA((blocks,)),
            pltpu.SemaphoreType.DMA((blocks,)),
            pltpu.SemaphoreType.DMA((ncols,)),
            pltpu.SemaphoreType.DMA((ncols,)),
        ],
        compiler_params=pltpu.CompilerParams(collective_id=0, has_side_effects=True),
    )(slip_delta, block_list, live_count, kernel)


def per_device(kernel, slip_delta, block_list, live_count, direct_effect, load_rate, time_before):
    nrows = lax.axis_size("rows")
    ncols = lax.axis_size("cols")
    stress_change = stress_sum(kernel, slip_delta, block_list, live_count, nrows, ncols)
    scale = direct_effect[:, None]
    growth = jnp.expm1(load_rate * time_before / direct_effect)[:, None]
    log_time = jnp.log(scale / load_rate[:, None]) + jnp.log(
        jnp.log1p(jnp.exp(-stress_change / scale) * growth)
    )
    return (stress_change, log_time)


def solution(mesh):
    in_specs = (
        P("rows", "cols"),
        P("cols", "rows", None),
        P("cols", "rows"),
        P("cols"),
        P(("rows", "cols")),
        P(("rows", "cols")),
        P(("rows", "cols")),
    )
    out_specs = (P(("rows", "cols"), None), P(("rows", "cols"), None))
    return jax.shard_map(
        per_device, mesh=mesh, in_specs=in_specs, out_specs=out_specs, check_vma=False
    )
```

```python
import functools

import jax
import jax.numpy as jnp
from jax import lax
from jax.experimental import pallas as pl
from jax.experimental.pallas import tpu as pltpu
from jax.sharding import PartitionSpec as P

BLOCK = 128
MESH = pl.DeviceIdType.MESH


def stress_kernel(nrows, ncols, groups, slip_ref, list_ref, count_ref, kernel_hbm, out_ref, pay_ref, kmat, gathered, dense_own,
                  landed, dense, sendbuf, slots, kload_sem, local_sem, g_send, g_recv, a_send, a_recv, r_send, r_recv, send_sem, recv_sem):
    me = lax.axis_index("cols")
    my_row = lax.axis_index("rows")
    share = out_ref.shape[0]
    per_group = ncols // groups
    here, list_here, patch = slip_ref.shape
    blocks = kmat.shape[1] // patch
    quarter = kmat.shape[0] // 4

    loads = []
    for q in range(4):
        load = pltpu.make_async_copy(
            kernel_hbm.at[pl.ds(q * quarter, quarter)], kmat.at[pl.ds(q * quarter, quarter)], kload_sem.at[q]
        )
        load.start()
        loads.append(load)

    pay_ref[0] = slip_ref[...]
    for e in range(here):
        for b in range(list_here):
            live = my_row * list_here + b < count_ref[e]
            key = jnp.where(live, list_ref[e, b], -1)
            pay_ref[1, e, pl.ds(b, 1), :] = jnp.full((1, patch), key, jnp.int32).astype(jnp.float32)

    barrier = pltpu.get_barrier_semaphore()
    for k in range(1, nrows):
        peer = lax.rem(my_row + k, nrows)
        pl.semaphore_signal(barrier, inc=1, device_id=(peer, me), device_id_type=MESH)
    for k in range(1, ncols):
        peer = lax.rem(me + k, ncols)
        pl.semaphore_signal(barrier, inc=1, device_id=(my_row, peer), device_id_type=MESH)
    pl.semaphore_wait(barrier, nrows + ncols - 2)

    def entries(r):
        return pl.ds(pl.multiple_of(r * list_here, list_here), list_here)

    sends = []
    a2a_sends = []
    for k in range(1, nrows):
        peer = lax.rem(my_row + k, nrows)
        copy = pltpu.make_async_remote_copy(
            src_ref=pay_ref,
            dst_ref=gathered.at[:, :, entries(my_row)],
            send_sem=g_send.at[peer],
            recv_sem=g_recv.at[my_row],
            device_id=(peer, me),
            device_id_type=MESH,
        )
        copy.start()
        sends.append(copy)
    local = pltpu.make_async_copy(pay_ref, gathered.at[:, :, entries(my_row)], local_sem)
    local.start()
    local.wait()
    for k in range(1, nrows):
        src = lax.rem(my_row + nrows - k, nrows)
        pltpu.make_async_remote_copy(
            src_ref=pay_ref,
            dst_ref=gathered.at[:, :, entries(src)],
            send_sem=g_send.at[src],
            recv_sem=g_recv.at[src],
            device_id=(src, me),
            device_id_type=MESH,
        ).wait_recv()

    total_blocks = dense_own.shape[1]
    lane = lax.broadcasted_iota(jnp.int32, (nrows * list_here, patch), 1)
    keys = [gathered[1, e].astype(jnp.int32) for e in range(here)]
    per_piece = patch // blocks
    for q in range(total_blocks // patch):
        for e in range(here):
            onehot = (keys[e] == lane + q * patch).astype(jnp.float32)
            dense_own[e, pl.ds(q * patch, patch), :] = lax.dot_general(
                onehot,
                gathered[0, e],
                (((0,), (0,)), ((), ())),
                precision=lax.Precision.HIGHEST,
                preferred_element_type=jnp.float32,
            )
        for i in range(per_piece):
            peer = q * per_piece + i
            copy = pltpu.make_async_remote_copy(
                src_ref=dense_own.at[:, pl.ds(peer * blocks, blocks)],
                dst_ref=landed.at[pl.ds(pl.multiple_of(me * here, here), here)],
                send_sem=a_send.at[peer],
                recv_sem=a_recv.at[me],
                device_id=(my_row, peer),
                device_id_type=MESH,
            )

            @pl.when(me != peer)
            def _():
                copy.start()

            a2a_sends.append((peer, copy))

    def mine(c):
        return pl.ds(pl.multiple_of(c * blocks, blocks), blocks)

    def slot(c):
        return pl.ds(pl.multiple_of(c * here, here), here)

    local = pltpu.make_async_copy(dense_own.at[:, mine(me)], landed.at[slot(me)], local_sem)
    local.start()
    local.wait()
    for k in range(1, ncols):
        src = lax.rem(me + ncols - k, ncols)
        pltpu.make_async_remote_copy(
            src_ref=dense_own.at[:, mine(src)],
            dst_ref=landed.at[slot(src)],
            send_sem=a_send.at[src],
            recv_sem=a_recv.at[src],
            device_id=(my_row, src),
            device_id_type=MESH,
        ).wait_recv()

    relayout = []
    for j in range(blocks):
        copy = pltpu.make_async_copy(landed.at[:, j], dense.at[j], r_send.at[j])
        copy.start()
        relayout.append(copy)
    for copy in relayout:
        copy.wait()
    for load in loads:
        load.wait()

    rs_sends = []
    for g in range(groups):
        rows = pl.ds(g * per_group * share, per_group * share)
        part = None
        for j in range(blocks):
            term = lax.dot_general(
                kmat[rows, pl.ds(j * patch, patch)],
                dense[j],
                (((1,), (1,)), ((), ())),
                precision=lax.Precision.HIGH,
                preferred_element_type=jnp.float32,
            )
            part = term if part is None else part + term
        for j in range(per_group):
            dest = g * per_group + j
            sendbuf[dest] = part[j * share:(j + 1) * share]
            copy = pltpu.make_async_remote_copy(
                src_ref=sendbuf.at[dest],
                dst_ref=slots.at[me],
                send_sem=send_sem.at[dest],
                recv_sem=recv_sem.at[me],
                device_id=(my_row, dest),
                device_id_type=MESH,
            )

            @pl.when(me != dest)
            def _():
                copy.start()

            rs_sends.append((dest, copy))

    total = sendbuf[me]
    for k in range(1, ncols):
        src = lax.rem(me + ncols - k, ncols)
        pltpu.make_async_remote_copy(
            src_ref=sendbuf.at[src],
            dst_ref=slots.at[src],
            send_sem=send_sem.at[src],
            recv_sem=recv_sem.at[src],
            device_id=(my_row, src),
            device_id_type=MESH,
        ).wait_recv()
        total = total + slots[src]
    out_ref[...] = total
    for copy in sends:
        copy.wait_send()
    for dest, copy in a2a_sends + rs_sends:

        @pl.when(me != dest)
        def _():
            copy.wait_send()


def stress_sum(kernel, slip_delta, block_list, live_count, nrows, ncols, groups=4):
    rows, sources = kernel.shape
    here, list_here, patch = slip_delta.shape
    events = ncols * here
    share = rows // ncols
    blocks = sources // patch
    return pl.pallas_call(
        functools.partial(stress_kernel, nrows, ncols, groups),
        out_shape=jax.ShapeDtypeStruct((share, events), jnp.float32),
        in_specs=[
            pl.BlockSpec(memory_space=pltpu.VMEM),
            pl.BlockSpec(memory_space=pltpu.SMEM),
            pl.BlockSpec(memory_space=pltpu.SMEM),
            pl.BlockSpec(memory_space=pl.ANY),
        ],
        out_specs=pl.BlockSpec(memory_space=pltpu.VMEM),
        scratch_shapes=[
            pltpu.VMEM((2, here, list_here, patch), jnp.float32),
            pltpu.VMEM((rows, sources), jnp.float32),
            pltpu.VMEM((2, here, nrows * list_here, patch), jnp.float32),
            pltpu.VMEM((here, ncols * blocks, patch), jnp.float32),
            pltpu.VMEM((events, blocks, patch), jnp.float32),
            pltpu.VMEM((blocks, events, patch), jnp.float32),
            pltpu.VMEM((ncols, share, events), jnp.float32),
            pltpu.VMEM((ncols, share, events), jnp.float32),
            pltpu.SemaphoreType.DMA((4,)),
            pltpu.SemaphoreType.DMA,
            pltpu.SemaphoreType.DMA((nrows,)),
            pltpu.SemaphoreType.DMA((nrows,)),
            pltpu.SemaphoreType.DMA((ncols,)),
            pltpu.SemaphoreType.DMA((ncols,)),
            pltpu.SemaphoreType.DMA((blocks,)),
            pltpu.SemaphoreType.DMA((blocks,)),
            pltpu.SemaphoreType.DMA((ncols,)),
            pltpu.SemaphoreType.DMA((ncols,)),
        ],
        compiler_params=pltpu.CompilerParams(collective_id=0, has_side_effects=True),
    )(slip_delta, block_list, live_count, kernel)


def per_device(kernel, slip_delta, block_list, live_count, direct_effect, load_rate, time_before):
    nrows = lax.axis_size("rows")
    ncols = lax.axis_size("cols")
    stress_change = stress_sum(kernel, slip_delta, block_list, live_count, nrows, ncols)
    scale = direct_effect[:, None]
    growth = jnp.expm1(load_rate * time_before / direct_effect)[:, None]
    log_time = jnp.log(scale / load_rate[:, None]) + jnp.log(
        jnp.log1p(jnp.exp(-stress_change / scale) * growth)
    )
    return (stress_change, log_time)


def solution(mesh):
    in_specs = (
        P("rows", "cols"),
        P("cols", "rows", None),
        P("cols", "rows"),
        P("cols"),
        P(("rows", "cols")),
        P(("rows", "cols")),
        P(("rows", "cols")),
    )
    out_specs = (P(("rows", "cols"), None), P(("rows", "cols"), None))
    return jax.shard_map(
        per_device, mesh=mesh, in_specs=in_specs, out_specs=out_specs, check_vma=False
    )
```

```python
import functools

import jax
import jax.numpy as jnp
from jax import lax
from jax.experimental import pallas as pl
from jax.experimental.pallas import tpu as pltpu
from jax.sharding import PartitionSpec as P

BLOCK = 128
MESH = pl.DeviceIdType.MESH


def stress_kernel(nrows, ncols, groups, slip_ref, list_ref, count_ref, kernel_hbm, out_ref, pay_ref, kmat, gathered, dense_own,
                  landed, dense, sendbuf, slots, kload_sem, local_sem, g_send, g_recv, a_send, a_recv, r_send, r_recv, send_sem, recv_sem):
    me = lax.axis_index("cols")
    my_row = lax.axis_index("rows")
    share = out_ref.shape[0]
    per_group = ncols // groups
    here, list_here, patch = slip_ref.shape
    blocks = kmat.shape[1] // patch
    quarter = kmat.shape[0] // 4

    loads = []
    for q in range(4):
        load = pltpu.make_async_copy(
            kernel_hbm.at[pl.ds(q * quarter, quarter)], kmat.at[pl.ds(q * quarter, quarter)], kload_sem.at[q]
        )
        load.start()
        loads.append(load)

    pay_ref[0] = slip_ref[...]
    for e in range(here):
        for b in range(list_here):
            live = my_row * list_here + b < count_ref[e]
            key = jnp.where(live, list_ref[e, b], -1)
            pay_ref[1, e, pl.ds(b, 1), :] = jnp.full((1, patch), key, jnp.int32).astype(jnp.float32)

    barrier = pltpu.get_barrier_semaphore()
    for k in range(1, nrows):
        peer = lax.rem(my_row + k, nrows)
        pl.semaphore_signal(barrier, inc=1, device_id=(peer, me), device_id_type=MESH)
    for k in range(1, ncols):
        peer = lax.rem(me + k, ncols)
        pl.semaphore_signal(barrier, inc=1, device_id=(my_row, peer), device_id_type=MESH)
    pl.semaphore_wait(barrier, nrows + ncols - 2)

    def entries(r):
        return pl.ds(pl.multiple_of(r * list_here, list_here), list_here)

    sends = []
    a2a_sends = []
    for k in range(1, nrows):
        peer = lax.rem(my_row + k, nrows)
        copy = pltpu.make_async_remote_copy(
            src_ref=pay_ref,
            dst_ref=gathered.at[:, :, entries(my_row)],
            send_sem=g_send.at[peer],
            recv_sem=g_recv.at[my_row],
            device_id=(peer, me),
            device_id_type=MESH,
        )
        copy.start()
        sends.append(copy)
    local = pltpu.make_async_copy(pay_ref, gathered.at[:, :, entries(my_row)], local_sem)
    local.start()
    local.wait()
    for k in range(1, nrows):
        src = lax.rem(my_row + nrows - k, nrows)
        pltpu.make_async_remote_copy(
            src_ref=pay_ref,
            dst_ref=gathered.at[:, :, entries(src)],
            send_sem=g_send.at[src],
            recv_sem=g_recv.at[src],
            device_id=(src, me),
            device_id_type=MESH,
        ).wait_recv()

    total_blocks = dense_own.shape[1]
    lane = lax.broadcasted_iota(jnp.int32, (nrows * list_here, patch), 1)
    keys = [gathered[1, e].astype(jnp.int32) for e in range(here)]
    per_piece = patch // blocks
    for q in range(total_blocks // patch):
        for e in range(here):
            onehot = (keys[e] == lane + q * patch).astype(jnp.float32)
            dense_own[e, pl.ds(q * patch, patch), :] = lax.dot_general(
                onehot,
                gathered[0, e],
                (((0,), (0,)), ((), ())),
                precision=lax.Precision.HIGHEST,
                preferred_element_type=jnp.float32,
            )
        for i in range(per_piece):
            peer = q * per_piece + i
            copy = pltpu.make_async_remote_copy(
                src_ref=dense_own.at[:, pl.ds(peer * blocks, blocks)],
                dst_ref=landed.at[pl.ds(pl.multiple_of(me * here, here), here)],
                send_sem=a_send.at[peer],
                recv_sem=a_recv.at[me],
                device_id=(my_row, peer),
                device_id_type=MESH,
            )

            @pl.when(me != peer)
            def _():
                copy.start()

            a2a_sends.append((peer, copy))

    def mine(c):
        return pl.ds(pl.multiple_of(c * blocks, blocks), blocks)

    def slot(c):
        return pl.ds(pl.multiple_of(c * here, here), here)

    local = pltpu.make_async_copy(dense_own.at[:, mine(me)], landed.at[slot(me)], local_sem)
    local.start()
    local.wait()
    for k in range(1, ncols):
        src = lax.rem(me + ncols - k, ncols)
        pltpu.make_async_remote_copy(
            src_ref=dense_own.at[:, mine(src)],
            dst_ref=landed.at[slot(src)],
            send_sem=a_send.at[src],
            recv_sem=a_recv.at[src],
            device_id=(my_row, src),
            device_id_type=MESH,
        ).wait_recv()

    relayout = []
    for j in range(blocks):
        copy = pltpu.make_async_copy(landed.at[:, j], dense.at[j], r_send.at[j])
        copy.start()
        relayout.append(copy)
    for copy in relayout:
        copy.wait()
    for load in loads:
        load.wait()

    rs_sends = []
    for g in range(groups):
        rows = pl.ds(g * per_group * share, per_group * share)
        part = None
        for j in range(blocks):
            term = lax.dot_general(
                kmat[rows, pl.ds(j * patch, patch)],
                dense[j],
                (((1,), (1,)), ((), ())),
                precision=lax.Precision.HIGH,
                preferred_element_type=jnp.float32,
            )
            part = term if part is None else part + term
        for j in range(per_group):
            dest = g * per_group + j
            sendbuf[dest] = part[j * share:(j + 1) * share]
            copy = pltpu.make_async_remote_copy(
                src_ref=sendbuf.at[dest],
                dst_ref=slots.at[me],
                send_sem=send_sem.at[dest],
                recv_sem=recv_sem.at[me],
                device_id=(my_row, dest),
                device_id_type=MESH,
            )

            @pl.when(me != dest)
            def _():
                copy.start()

            rs_sends.append((dest, copy))

    total = sendbuf[me]
    for k in range(1, ncols):
        src = lax.rem(me + ncols - k, ncols)
        pltpu.make_async_remote_copy(
            src_ref=sendbuf.at[src],
            dst_ref=slots.at[src],
            send_sem=send_sem.at[src],
            recv_sem=recv_sem.at[src],
            device_id=(my_row, src),
            device_id_type=MESH,
        ).wait_recv()
        total = total + slots[src]
    out_ref[...] = total
    for copy in sends:
        copy.wait_send()
    for dest, copy in a2a_sends + rs_sends:

        @pl.when(me != dest)
        def _():
            copy.wait_send()


def stress_sum(kernel, slip_delta, block_list, live_count, nrows, ncols, groups=4):
    rows, sources = kernel.shape
    here, list_here, patch = slip_delta.shape
    events = ncols * here
    share = rows // ncols
    blocks = sources // patch
    return pl.pallas_call(
        functools.partial(stress_kernel, nrows, ncols, groups),
        out_shape=jax.ShapeDtypeStruct((share, events), jnp.float32),
        in_specs=[
            pl.BlockSpec(memory_space=pltpu.VMEM),
            pl.BlockSpec(memory_space=pltpu.SMEM),
            pl.BlockSpec(memory_space=pltpu.SMEM),
            pl.BlockSpec(memory_space=pl.ANY),
        ],
        out_specs=pl.BlockSpec(memory_space=pltpu.VMEM),
        scratch_shapes=[
            pltpu.VMEM((2, here, list_here, patch), jnp.float32),
            pltpu.VMEM((rows, sources), jnp.float32),
            pltpu.VMEM((2, here, nrows * list_here, patch), jnp.float32),
            pltpu.VMEM((here, ncols * blocks, patch), jnp.float32),
            pltpu.VMEM((events, blocks, patch), jnp.float32),
            pltpu.VMEM((blocks, events, patch), jnp.float32),
            pltpu.VMEM((ncols, share, events), jnp.float32),
            pltpu.VMEM((ncols, share, events), jnp.float32),
            pltpu.SemaphoreType.DMA((4,)),
            pltpu.SemaphoreType.DMA,
            pltpu.SemaphoreType.DMA((nrows,)),
            pltpu.SemaphoreType.DMA((nrows,)),
            pltpu.SemaphoreType.DMA((ncols,)),
            pltpu.SemaphoreType.DMA((ncols,)),
            pltpu.SemaphoreType.DMA((blocks,)),
            pltpu.SemaphoreType.DMA((blocks,)),
            pltpu.SemaphoreType.DMA((ncols,)),
            pltpu.SemaphoreType.DMA((ncols,)),
        ],
        compiler_params=pltpu.CompilerParams(collective_id=0, has_side_effects=True),
    )(slip_delta, block_list, live_count, kernel)


def epilogue_kernel(stress_ref, scale_ref, offset_ref, growth_ref, out_ref, log_ref):
    stress = stress_ref[...]
    row = lax.broadcasted_iota(jnp.int32, stress.shape, 0)
    scale = jnp.zeros_like(stress)
    offset = jnp.zeros_like(stress)
    growth = jnp.zeros_like(stress)
    for i in range(stress.shape[0]):
        pick = row == i
        scale = jnp.where(pick, scale_ref[i], scale)
        offset = jnp.where(pick, offset_ref[i], offset)
        growth = jnp.where(pick, growth_ref[i], growth)
    out_ref[...] = stress
    log_ref[...] = offset + jnp.log(jnp.log1p(jnp.exp(-stress / scale) * growth))


def epilogue(stress, scale, offset, growth):
    shape = jax.ShapeDtypeStruct(stress.shape, jnp.float32)
    return pl.pallas_call(
        epilogue_kernel,
        out_shape=(shape, shape),
        in_specs=[pl.BlockSpec(memory_space=pltpu.VMEM)] + [pl.BlockSpec(memory_space=pltpu.SMEM)] * 3,
        out_specs=(pl.BlockSpec(memory_space=pltpu.VMEM), pl.BlockSpec(memory_space=pltpu.VMEM)),
    )(stress, scale, offset, growth)


def per_device(kernel, slip_delta, block_list, live_count, direct_effect, load_rate, time_before):
    nrows = lax.axis_size("rows")
    ncols = lax.axis_size("cols")
    stress_change = stress_sum(kernel, slip_delta, block_list, live_count, nrows, ncols)
    offset = jnp.log(direct_effect / load_rate)
    growth = jnp.expm1(load_rate * time_before / direct_effect)
    return epilogue(stress_change, direct_effect, offset, growth)


def solution(mesh):
    in_specs = (
        P("rows", "cols"),
        P("cols", "rows", None),
        P("cols", "rows"),
        P("cols"),
        P(("rows", "cols")),
        P(("rows", "cols")),
        P(("rows", "cols")),
    )
    out_specs = (P(("rows", "cols"), None), P(("rows", "cols"), None))
    return jax.shard_map(
        per_device, mesh=mesh, in_specs=in_specs, out_specs=out_specs, check_vma=False
    )
```

```python
import functools

import jax
import jax.numpy as jnp
from jax import lax
from jax.experimental import pallas as pl
from jax.experimental.pallas import tpu as pltpu
from jax.sharding import PartitionSpec as P

BLOCK = 128
MESH = pl.DeviceIdType.MESH


def stress_kernel(nrows, ncols, groups, slip_ref, list_ref, count_ref, kernel_hbm, out_ref, pay_ref, kmat, gathered, dense_own,
                  landed, dense, sendbuf, slots, kload_sem, local_sem, g_send, g_recv, a_send, a_recv, r_send, r_recv, send_sem, recv_sem):
    me = lax.axis_index("cols")
    my_row = lax.axis_index("rows")
    share = out_ref.shape[0]
    per_group = ncols // groups
    here, list_here, patch = slip_ref.shape
    blocks = kmat.shape[1] // patch
    quarter = kmat.shape[0] // 4

    loads = []
    for q in range(4):
        load = pltpu.make_async_copy(
            kernel_hbm.at[pl.ds(q * quarter, quarter)], kmat.at[pl.ds(q * quarter, quarter)], kload_sem.at[q]
        )
        load.start()
        loads.append(load)

    pay_ref[0] = slip_ref[...]
    for e in range(here):
        for b in range(list_here):
            live = my_row * list_here + b < count_ref[e]
            key = jnp.where(live, list_ref[e, b], -1)
            pay_ref[1, e, pl.ds(b, 1), :] = jnp.full((1, patch), key, jnp.int32).astype(jnp.float32)

    barrier = pltpu.get_barrier_semaphore()
    for k in range(1, nrows):
        peer = lax.rem(my_row + k, nrows)
        pl.semaphore_signal(barrier, inc=1, device_id=(peer, me), device_id_type=MESH)
    for k in range(1, ncols):
        peer = lax.rem(me + k, ncols)
        pl.semaphore_signal(barrier, inc=1, device_id=(my_row, peer), device_id_type=MESH)
    pl.semaphore_wait(barrier, nrows + ncols - 2)

    def entries(r):
        return pl.ds(pl.multiple_of(r * list_here, list_here), list_here)

    sends = []
    a2a_sends = []
    for k in range(1, nrows):
        peer = lax.rem(my_row + k, nrows)
        copy = pltpu.make_async_remote_copy(
            src_ref=pay_ref,
            dst_ref=gathered.at[:, :, entries(my_row)],
            send_sem=g_send.at[peer],
            recv_sem=g_recv.at[my_row],
            device_id=(peer, me),
            device_id_type=MESH,
        )
        copy.start()
        sends.append(copy)
    local = pltpu.make_async_copy(pay_ref, gathered.at[:, :, entries(my_row)], local_sem)
    local.start()
    local.wait()
    for k in range(1, nrows):
        src = lax.rem(my_row + nrows - k, nrows)
        pltpu.make_async_remote_copy(
            src_ref=pay_ref,
            dst_ref=gathered.at[:, :, entries(src)],
            send_sem=g_send.at[src],
            recv_sem=g_recv.at[src],
            device_id=(src, me),
            device_id_type=MESH,
        ).wait_recv()

    total_blocks = dense_own.shape[1]
    lane = lax.broadcasted_iota(jnp.int32, (nrows * list_here, patch), 1)
    keys = [gathered[1, e].astype(jnp.int32) for e in range(here)]
    per_piece = patch // blocks
    for q in range(total_blocks // patch):
        for e in range(here):
            onehot = (keys[e] == lane + q * patch).astype(jnp.float32)
            dense_own[e, pl.ds(q * patch, patch), :] = lax.dot_general(
                onehot,
                gathered[0, e],
                (((0,), (0,)), ((), ())),
                precision=lax.Precision.HIGHEST,
                preferred_element_type=jnp.float32,
            )
        for i in range(per_piece):
            peer = q * per_piece + i
            copy = pltpu.make_async_remote_copy(
                src_ref=dense_own.at[:, pl.ds(peer * blocks, blocks)],
                dst_ref=landed.at[pl.ds(pl.multiple_of(me * here, here), here)],
                send_sem=a_send.at[peer],
                recv_sem=a_recv.at[me],
                device_id=(my_row, peer),
                device_id_type=MESH,
            )

            @pl.when(me != peer)
            def _():
                copy.start()

            a2a_sends.append((peer, copy))

    def mine(c):
        return pl.ds(pl.multiple_of(c * blocks, blocks), blocks)

    def slot(c):
        return pl.ds(pl.multiple_of(c * here, here), here)

    local = pltpu.make_async_copy(dense_own.at[:, mine(me)], landed.at[slot(me)], local_sem)
    local.start()
    local.wait()
    for k in range(1, ncols):
        src = lax.rem(me + ncols - k, ncols)
        pltpu.make_async_remote_copy(
            src_ref=dense_own.at[:, mine(src)],
            dst_ref=landed.at[slot(src)],
            send_sem=a_send.at[src],
            recv_sem=a_recv.at[src],
            device_id=(my_row, src),
            device_id_type=MESH,
        ).wait_recv()

    relayout = []
    for j in range(blocks):
        copy = pltpu.make_async_copy(landed.at[:, j], dense.at[j], r_send.at[j])
        copy.start()
        relayout.append(copy)
    for copy in relayout:
        copy.wait()
    for load in loads:
        load.wait()

    rs_sends = []
    for g in range(groups):
        rows = pl.ds(g * per_group * share, per_group * share)
        part = None
        for j in range(blocks):
            term = lax.dot_general(
                kmat[rows, pl.ds(j * patch, patch)],
                dense[j],
                (((1,), (1,)), ((), ())),
                precision=lax.Precision.HIGH,
                preferred_element_type=jnp.float32,
            )
            part = term if part is None else part + term
        for j in range(per_group):
            dest = g * per_group + j
            sendbuf[dest] = part[j * share:(j + 1) * share]
            copy = pltpu.make_async_remote_copy(
                src_ref=sendbuf.at[dest],
                dst_ref=slots.at[me],
                send_sem=send_sem.at[dest],
                recv_sem=recv_sem.at[me],
                device_id=(my_row, dest),
                device_id_type=MESH,
            )

            @pl.when(me != dest)
            def _():
                copy.start()

            rs_sends.append((dest, copy))

    total = sendbuf[me]
    for k in range(1, ncols):
        src = lax.rem(me + ncols - k, ncols)
        pltpu.make_async_remote_copy(
            src_ref=sendbuf.at[src],
            dst_ref=slots.at[src],
            send_sem=send_sem.at[src],
            recv_sem=recv_sem.at[src],
            device_id=(my_row, src),
            device_id_type=MESH,
        ).wait_recv()
        total = total + slots[src]
    out_ref[...] = total
    for copy in sends:
        copy.wait_send()
    for dest, copy in a2a_sends + rs_sends:

        @pl.when(me != dest)
        def _():
            copy.wait_send()


def stress_sum(kernel, slip_delta, block_list, live_count, nrows, ncols, groups=4):
    rows, sources = kernel.shape
    here, list_here, patch = slip_delta.shape
    events = ncols * here
    share = rows // ncols
    blocks = sources // patch
    return pl.pallas_call(
        functools.partial(stress_kernel, nrows, ncols, groups),
        out_shape=jax.ShapeDtypeStruct((share, events), jnp.float32),
        in_specs=[
            pl.BlockSpec(memory_space=pltpu.VMEM),
            pl.BlockSpec(memory_space=pltpu.SMEM),
            pl.BlockSpec(memory_space=pltpu.SMEM),
            pl.BlockSpec(memory_space=pl.ANY),
        ],
        out_specs=pl.BlockSpec(memory_space=pltpu.VMEM),
        scratch_shapes=[
            pltpu.VMEM((2, here, list_here, patch), jnp.float32),
            pltpu.VMEM((rows, sources), jnp.float32),
            pltpu.VMEM((2, here, nrows * list_here, patch), jnp.float32),
            pltpu.VMEM((here, ncols * blocks, patch), jnp.float32),
            pltpu.VMEM((events, blocks, patch), jnp.float32),
            pltpu.VMEM((blocks, events, patch), jnp.float32),
            pltpu.VMEM((ncols, share, events), jnp.float32),
            pltpu.VMEM((ncols, share, events), jnp.float32),
            pltpu.SemaphoreType.DMA((4,)),
            pltpu.SemaphoreType.DMA,
            pltpu.SemaphoreType.DMA((nrows,)),
            pltpu.SemaphoreType.DMA((nrows,)),
            pltpu.SemaphoreType.DMA((ncols,)),
            pltpu.SemaphoreType.DMA((ncols,)),
            pltpu.SemaphoreType.DMA((blocks,)),
            pltpu.SemaphoreType.DMA((blocks,)),
            pltpu.SemaphoreType.DMA((ncols,)),
            pltpu.SemaphoreType.DMA((ncols,)),
        ],
        compiler_params=pltpu.CompilerParams(collective_id=0, has_side_effects=True),
    )(slip_delta, block_list, live_count, kernel)


def epilogue_kernel(stress_ref, scale_ref, rate_ref, before_ref, out_ref, log_ref):
    stress = stress_ref[...]
    row = lax.broadcasted_iota(jnp.int32, stress.shape, 0)
    scale = jnp.ones_like(stress)
    rate = jnp.ones_like(stress)
    before = jnp.ones_like(stress)
    for i in range(stress.shape[0]):
        pick = row == i
        scale = jnp.where(pick, scale_ref[i], scale)
        rate = jnp.where(pick, rate_ref[i], rate)
        before = jnp.where(pick, before_ref[i], before)
    x = rate * before / scale
    u = jnp.exp(x)
    growth = jnp.where(u == 1.0, x, (u - 1.0) * x / jnp.log(u))
    out_ref[...] = stress
    log_ref[...] = jnp.log(scale / rate) + jnp.log(jnp.log1p(jnp.exp(-stress / scale) * growth))


def epilogue(stress, scale, rate, before):
    shape = jax.ShapeDtypeStruct(stress.shape, jnp.float32)
    return pl.pallas_call(
        epilogue_kernel,
        out_shape=(shape, shape),
        in_specs=[pl.BlockSpec(memory_space=pltpu.VMEM)] + [pl.BlockSpec(memory_space=pltpu.SMEM)] * 3,
        out_specs=(pl.BlockSpec(memory_space=pltpu.VMEM), pl.BlockSpec(memory_space=pltpu.VMEM)),
    )(stress, scale, rate, before)


def per_device(kernel, slip_delta, block_list, live_count, direct_effect, load_rate, time_before):
    nrows = lax.axis_size("rows")
    ncols = lax.axis_size("cols")
    stress_change = stress_sum(kernel, slip_delta, block_list, live_count, nrows, ncols)
    return epilogue(stress_change, direct_effect, load_rate, time_before)


def solution(mesh):
    in_specs = (
        P("rows", "cols"),
        P("cols", "rows", None),
        P("cols", "rows"),
        P("cols"),
        P(("rows", "cols")),
        P(("rows", "cols")),
        P(("rows", "cols")),
    )
    out_specs = (P(("rows", "cols"), None), P(("rows", "cols"), None))
    return jax.shard_map(
        per_device, mesh=mesh, in_specs=in_specs, out_specs=out_specs, check_vma=False
    )
```

```python
import functools

import jax
import jax.numpy as jnp
from jax import lax
from jax.experimental import pallas as pl
from jax.experimental.pallas import tpu as pltpu
from jax.sharding import PartitionSpec as P

BLOCK = 128
MESH = pl.DeviceIdType.MESH


def stress_kernel(nrows, ncols, groups, slip_ref, list_ref, count_ref, kernel_hbm, out_ref, pay_ref, kmat, gathered, dense_own,
                  landed, dense, sendbuf, slots, kload_sem, local_sem, g_send, g_recv, a_send, a_recv, r_send, r_recv, send_sem, recv_sem):
    me = lax.axis_index("cols")
    my_row = lax.axis_index("rows")
    share = out_ref.shape[0]
    per_group = ncols // groups
    here, list_here, patch = slip_ref.shape
    blocks = kmat.shape[1] // patch
    quarter = kmat.shape[0] // 4

    pay_ref[0] = slip_ref[...]
    for e in range(here):
        for b in range(list_here):
            live = my_row * list_here + b < count_ref[e]
            key = jnp.where(live, list_ref[e, b], -1)
            pay_ref[1, e, pl.ds(b, 1), :] = jnp.full((1, patch), key, jnp.int32).astype(jnp.float32)

    barrier = pltpu.get_barrier_semaphore()
    for k in range(1, nrows):
        peer = lax.rem(my_row + k, nrows)
        pl.semaphore_signal(barrier, inc=1, device_id=(peer, me), device_id_type=MESH)
    for k in range(1, ncols):
        peer = lax.rem(me + k, ncols)
        pl.semaphore_signal(barrier, inc=1, device_id=(my_row, peer), device_id_type=MESH)
    pl.semaphore_wait(barrier, nrows + ncols - 2)

    def entries(r):
        return pl.ds(pl.multiple_of(r * list_here, list_here), list_here)

    sends = []
    a2a_sends = []
    for k in range(1, nrows):
        peer = lax.rem(my_row + k, nrows)
        copy = pltpu.make_async_remote_copy(
            src_ref=pay_ref,
            dst_ref=gathered.at[:, :, entries(my_row)],
            send_sem=g_send.at[peer],
            recv_sem=g_recv.at[my_row],
            device_id=(peer, me),
            device_id_type=MESH,
        )
        copy.start()
        sends.append(copy)
    local = pltpu.make_async_copy(pay_ref, gathered.at[:, :, entries(my_row)], local_sem)
    local.start()
    local.wait()
    for k in range(1, nrows):
        src = lax.rem(my_row + nrows - k, nrows)
        pltpu.make_async_remote_copy(
            src_ref=pay_ref,
            dst_ref=gathered.at[:, :, entries(src)],
            send_sem=g_send.at[src],
            recv_sem=g_recv.at[src],
            device_id=(src, me),
            device_id_type=MESH,
        ).wait_recv()

    total_blocks = dense_own.shape[1]
    lane = lax.broadcasted_iota(jnp.int32, (nrows * list_here, patch), 1)
    keys = [gathered[1, e].astype(jnp.int32) for e in range(here)]
    per_piece = patch // blocks
    for q in range(total_blocks // patch):
        for e in range(here):
            onehot = (keys[e] == lane + q * patch).astype(jnp.float32)
            dense_own[e, pl.ds(q * patch, patch), :] = lax.dot_general(
                onehot,
                gathered[0, e],
                (((0,), (0,)), ((), ())),
                precision=lax.Precision.HIGHEST,
                preferred_element_type=jnp.float32,
            )
        for i in range(per_piece):
            peer = q * per_piece + i
            copy = pltpu.make_async_remote_copy(
                src_ref=dense_own.at[:, pl.ds(peer * blocks, blocks)],
                dst_ref=landed.at[pl.ds(pl.multiple_of(me * here, here), here)],
                send_sem=a_send.at[peer],
                recv_sem=a_recv.at[me],
                device_id=(my_row, peer),
                device_id_type=MESH,
            )

            @pl.when(me != peer)
            def _():
                copy.start()

            a2a_sends.append((peer, copy))

    loads = []
    for q in range(4):
        load = pltpu.make_async_copy(
            kernel_hbm.at[pl.ds(q * quarter, quarter)], kmat.at[pl.ds(q * quarter, quarter)], kload_sem.at[q]
        )
        load.start()
        loads.append(load)

    def mine(c):
        return pl.ds(pl.multiple_of(c * blocks, blocks), blocks)

    def slot(c):
        return pl.ds(pl.multiple_of(c * here, here), here)

    local = pltpu.make_async_copy(dense_own.at[:, mine(me)], landed.at[slot(me)], local_sem)
    local.start()
    local.wait()
    for k in range(1, ncols):
        src = lax.rem(me + ncols - k, ncols)
        pltpu.make_async_remote_copy(
            src_ref=dense_own.at[:, mine(src)],
            dst_ref=landed.at[slot(src)],
            send_sem=a_send.at[src],
            recv_sem=a_recv.at[src],
            device_id=(my_row, src),
            device_id_type=MESH,
        ).wait_recv()

    relayout = []
    for j in range(blocks):
        copy = pltpu.make_async_copy(landed.at[:, j], dense.at[j], r_send.at[j])
        copy.start()
        relayout.append(copy)
    for copy in relayout:
        copy.wait()
    for load in loads:
        load.wait()

    rs_sends = []
    for g in range(groups):
        rows = pl.ds(g * per_group * share, per_group * share)
        part = None
        for j in range(blocks):
            term = lax.dot_general(
                kmat[rows, pl.ds(j * patch, patch)],
                dense[j],
                (((1,), (1,)), ((), ())),
                precision=lax.Precision.HIGH,
                preferred_element_type=jnp.float32,
            )
            part = term if part is None else part + term
        for j in range(per_group):
            dest = g * per_group + j
            sendbuf[dest] = part[j * share:(j + 1) * share]
            copy = pltpu.make_async_remote_copy(
                src_ref=sendbuf.at[dest],
                dst_ref=slots.at[me],
                send_sem=send_sem.at[dest],
                recv_sem=recv_sem.at[me],
                device_id=(my_row, dest),
                device_id_type=MESH,
            )

            @pl.when(me != dest)
            def _():
                copy.start()

            rs_sends.append((dest, copy))

    total = sendbuf[me]
    for k in range(1, ncols):
        src = lax.rem(me + ncols - k, ncols)
        pltpu.make_async_remote_copy(
            src_ref=sendbuf.at[src],
            dst_ref=slots.at[src],
            send_sem=send_sem.at[src],
            recv_sem=recv_sem.at[src],
            device_id=(my_row, src),
            device_id_type=MESH,
        ).wait_recv()
        total = total + slots[src]
    out_ref[...] = total
    for copy in sends:
        copy.wait_send()
    for dest, copy in a2a_sends + rs_sends:

        @pl.when(me != dest)
        def _():
            copy.wait_send()


def stress_sum(kernel, slip_delta, block_list, live_count, nrows, ncols, groups=4):
    rows, sources = kernel.shape
    here, list_here, patch = slip_delta.shape
    events = ncols * here
    share = rows // ncols
    blocks = sources // patch
    return pl.pallas_call(
        functools.partial(stress_kernel, nrows, ncols, groups),
        out_shape=jax.ShapeDtypeStruct((share, events), jnp.float32),
        in_specs=[
            pl.BlockSpec(memory_space=pltpu.VMEM),
            pl.BlockSpec(memory_space=pltpu.SMEM),
            pl.BlockSpec(memory_space=pltpu.SMEM),
            pl.BlockSpec(memory_space=pl.ANY),
        ],
        out_specs=pl.BlockSpec(memory_space=pltpu.VMEM),
        scratch_shapes=[
            pltpu.VMEM((2, here, list_here, patch), jnp.float32),
            pltpu.VMEM((rows, sources), jnp.float32),
            pltpu.VMEM((2, here, nrows * list_here, patch), jnp.float32),
            pltpu.VMEM((here, ncols * blocks, patch), jnp.float32),
            pltpu.VMEM((events, blocks, patch), jnp.float32),
            pltpu.VMEM((blocks, events, patch), jnp.float32),
            pltpu.VMEM((ncols, share, events), jnp.float32),
            pltpu.VMEM((ncols, share, events), jnp.float32),
            pltpu.SemaphoreType.DMA((4,)),
            pltpu.SemaphoreType.DMA,
            pltpu.SemaphoreType.DMA((nrows,)),
            pltpu.SemaphoreType.DMA((nrows,)),
            pltpu.SemaphoreType.DMA((ncols,)),
            pltpu.SemaphoreType.DMA((ncols,)),
            pltpu.SemaphoreType.DMA((blocks,)),
            pltpu.SemaphoreType.DMA((blocks,)),
            pltpu.SemaphoreType.DMA((ncols,)),
            pltpu.SemaphoreType.DMA((ncols,)),
        ],
        compiler_params=pltpu.CompilerParams(collective_id=0, has_side_effects=True),
    )(slip_delta, block_list, live_count, kernel)


def epilogue_kernel(stress_ref, scale_ref, rate_ref, before_ref, out_ref, log_ref):
    stress = stress_ref[...]
    row = lax.broadcasted_iota(jnp.int32, stress.shape, 0)
    scale = jnp.ones_like(stress)
    rate = jnp.ones_like(stress)
    before = jnp.ones_like(stress)
    for i in range(stress.shape[0]):
        pick = row == i
        scale = jnp.where(pick, scale_ref[i], scale)
        rate = jnp.where(pick, rate_ref[i], rate)
        before = jnp.where(pick, before_ref[i], before)
    x = rate * before / scale
    u = jnp.exp(x)
    growth = jnp.where(u == 1.0, x, (u - 1.0) * x / jnp.log(u))
    out_ref[...] = stress
    log_ref[...] = jnp.log(scale / rate) + jnp.log(jnp.log1p(jnp.exp(-stress / scale) * growth))


def epilogue(stress, scale, rate, before):
    shape = jax.ShapeDtypeStruct(stress.shape, jnp.float32)
    return pl.pallas_call(
        epilogue_kernel,
        out_shape=(shape, shape),
        in_specs=[pl.BlockSpec(memory_space=pltpu.VMEM)] + [pl.BlockSpec(memory_space=pltpu.SMEM)] * 3,
        out_specs=(pl.BlockSpec(memory_space=pltpu.VMEM), pl.BlockSpec(memory_space=pltpu.VMEM)),
    )(stress, scale, rate, before)


def per_device(kernel, slip_delta, block_list, live_count, direct_effect, load_rate, time_before):
    nrows = lax.axis_size("rows")
    ncols = lax.axis_size("cols")
    stress_change = stress_sum(kernel, slip_delta, block_list, live_count, nrows, ncols)
    return epilogue(stress_change, direct_effect, load_rate, time_before)


def solution(mesh):
    in_specs = (
        P("rows", "cols"),
        P("cols", "rows", None),
        P("cols", "rows"),
        P("cols"),
        P(("rows", "cols")),
        P(("rows", "cols")),
        P(("rows", "cols")),
    )
    out_specs = (P(("rows", "cols"), None), P(("rows", "cols"), None))
    return jax.shard_map(
        per_device, mesh=mesh, in_specs=in_specs, out_specs=out_specs, check_vma=False
    )
```

```python
import functools

import jax
import jax.numpy as jnp
from jax import lax
from jax.experimental import pallas as pl
from jax.experimental.pallas import tpu as pltpu
from jax.sharding import PartitionSpec as P

BLOCK = 128
MESH = pl.DeviceIdType.MESH


def stress_kernel(nrows, ncols, groups, slip_ref, list_ref, count_ref, kernel_hbm, out_ref, pay_ref, kmat, gathered, dense_own,
                  landed, dense, sendbuf, slots, kload_sem, local_sem, g_send, g_recv, a_send, a_recv, r_send, r_recv, send_sem, recv_sem):
    me = lax.axis_index("cols")
    my_row = lax.axis_index("rows")
    share = out_ref.shape[0]
    per_group = ncols // groups
    here, list_here, patch = slip_ref.shape
    blocks = kmat.shape[1] // patch
    quarter = kmat.shape[0] // 4

    pay_ref[0] = slip_ref[...]
    for e in range(here):
        for b in range(list_here):
            live = my_row * list_here + b < count_ref[e]
            key = jnp.where(live, list_ref[e, b], -1)
            pay_ref[1, e, pl.ds(b, 1), :] = jnp.full((1, patch), key, jnp.int32).astype(jnp.float32)

    barrier = pltpu.get_barrier_semaphore()
    for k in range(1, nrows):
        peer = lax.rem(my_row + k, nrows)
        pl.semaphore_signal(barrier, inc=1, device_id=(peer, me), device_id_type=MESH)
    for k in range(1, ncols):
        peer = lax.rem(me + k, ncols)
        pl.semaphore_signal(barrier, inc=1, device_id=(my_row, peer), device_id_type=MESH)
    pl.semaphore_wait(barrier, nrows + ncols - 2)

    def entries(r):
        return pl.ds(pl.multiple_of(r * list_here, list_here), list_here)

    sends = []
    a2a_sends = []
    for k in range(1, nrows):
        peer = lax.rem(my_row + k, nrows)
        copy = pltpu.make_async_remote_copy(
            src_ref=pay_ref,
            dst_ref=gathered.at[:, :, entries(my_row)],
            send_sem=g_send.at[peer],
            recv_sem=g_recv.at[my_row],
            device_id=(peer, me),
            device_id_type=MESH,
        )
        copy.start()
        sends.append(copy)
    local = pltpu.make_async_copy(pay_ref, gathered.at[:, :, entries(my_row)], local_sem)
    local.start()
    local.wait()
    for k in range(1, nrows):
        src = lax.rem(my_row + nrows - k, nrows)
        pltpu.make_async_remote_copy(
            src_ref=pay_ref,
            dst_ref=gathered.at[:, :, entries(src)],
            send_sem=g_send.at[src],
            recv_sem=g_recv.at[src],
            device_id=(src, me),
            device_id_type=MESH,
        ).wait_recv()

    total_blocks = dense_own.shape[1]
    lane = lax.broadcasted_iota(jnp.int32, (nrows * list_here, patch), 1)
    keys = [gathered[1, e].astype(jnp.int32) for e in range(here)]
    per_piece = patch // blocks
    for q in range(total_blocks // patch):
        for e in range(here):
            onehot = (keys[e] == lane + q * patch).astype(jnp.float32)
            dense_own[e, pl.ds(q * patch, patch), :] = lax.dot_general(
                onehot,
                gathered[0, e],
                (((0,), (0,)), ((), ())),
                precision=lax.Precision.HIGHEST,
                preferred_element_type=jnp.float32,
            )
        for i in range(per_piece):
            peer = q * per_piece + i
            copy = pltpu.make_async_remote_copy(
                src_ref=dense_own.at[:, pl.ds(peer * blocks, blocks)],
                dst_ref=landed.at[pl.ds(pl.multiple_of(me * here, here), here)],
                send_sem=a_send.at[peer],
                recv_sem=a_recv.at[me],
                device_id=(my_row, peer),
                device_id_type=MESH,
            )

            @pl.when(me != peer)
            def _():
                copy.start()

            a2a_sends.append((peer, copy))

    loads = []
    for q in range(4):
        load = pltpu.make_async_copy(
            kernel_hbm.at[pl.ds(q * quarter, quarter)], kmat.at[pl.ds(q * quarter, quarter)], kload_sem.at[q]
        )
        load.start()
        loads.append(load)

    def mine(c):
        return pl.ds(pl.multiple_of(c * blocks, blocks), blocks)

    def slot(c):
        return pl.ds(pl.multiple_of(c * here, here), here)

    local = pltpu.make_async_copy(dense_own.at[:, mine(me)], landed.at[slot(me)], local_sem)
    local.start()
    local.wait()
    for k in range(1, ncols):
        src = lax.rem(me + ncols - k, ncols)
        pltpu.make_async_remote_copy(
            src_ref=dense_own.at[:, mine(src)],
            dst_ref=landed.at[slot(src)],
            send_sem=a_send.at[src],
            recv_sem=a_recv.at[src],
            device_id=(my_row, src),
            device_id_type=MESH,
        ).wait_recv()

    relayout = []
    for j in range(blocks):
        copy = pltpu.make_async_copy(landed.at[:, j], dense.at[j], r_send.at[j])
        copy.start()
        relayout.append(copy)
    for copy in relayout:
        copy.wait()
    for load in loads:
        load.wait()

    rs_sends = []
    for g in range(groups):
        rows = pl.ds(g * per_group * share, per_group * share)
        part = None
        for j in range(blocks):
            term = lax.dot_general(
                kmat[rows, pl.ds(j * patch, patch)],
                dense[j],
                (((1,), (1,)), ((), ())),
                precision=lax.Precision.HIGH,
                preferred_element_type=jnp.float32,
            )
            part = term if part is None else part + term
        for j in range(per_group):
            dest = g * per_group + j
            sendbuf[dest] = part[j * share:(j + 1) * share]
            copy = pltpu.make_async_remote_copy(
                src_ref=sendbuf.at[dest],
                dst_ref=slots.at[me],
                send_sem=send_sem.at[dest],
                recv_sem=recv_sem.at[me],
                device_id=(my_row, dest),
                device_id_type=MESH,
            )

            @pl.when(me != dest)
            def _():
                copy.start()

            rs_sends.append((dest, copy))

    total = sendbuf[me]
    for k in range(1, ncols):
        src = lax.rem(me + ncols - k, ncols)
        pltpu.make_async_remote_copy(
            src_ref=sendbuf.at[src],
            dst_ref=slots.at[src],
            send_sem=send_sem.at[src],
            recv_sem=recv_sem.at[src],
            device_id=(my_row, src),
            device_id_type=MESH,
        ).wait_recv()
        total = total + slots[src]
    out_ref[...] = total
    for copy in sends:
        copy.wait_send()
    for dest, copy in a2a_sends + rs_sends:

        @pl.when(me != dest)
        def _():
            copy.wait_send()


def stress_sum(kernel, slip_delta, block_list, live_count, nrows, ncols, groups=8):
    rows, sources = kernel.shape
    here, list_here, patch = slip_delta.shape
    events = ncols * here
    share = rows // ncols
    blocks = sources // patch
    return pl.pallas_call(
        functools.partial(stress_kernel, nrows, ncols, groups),
        out_shape=jax.ShapeDtypeStruct((share, events), jnp.float32),
        in_specs=[
            pl.BlockSpec(memory_space=pltpu.VMEM),
            pl.BlockSpec(memory_space=pltpu.SMEM),
            pl.BlockSpec(memory_space=pltpu.SMEM),
            pl.BlockSpec(memory_space=pl.ANY),
        ],
        out_specs=pl.BlockSpec(memory_space=pltpu.VMEM),
        scratch_shapes=[
            pltpu.VMEM((2, here, list_here, patch), jnp.float32),
            pltpu.VMEM((rows, sources), jnp.float32),
            pltpu.VMEM((2, here, nrows * list_here, patch), jnp.float32),
            pltpu.VMEM((here, ncols * blocks, patch), jnp.float32),
            pltpu.VMEM((events, blocks, patch), jnp.float32),
            pltpu.VMEM((blocks, events, patch), jnp.float32),
            pltpu.VMEM((ncols, share, events), jnp.float32),
            pltpu.VMEM((ncols, share, events), jnp.float32),
            pltpu.SemaphoreType.DMA((4,)),
            pltpu.SemaphoreType.DMA,
            pltpu.SemaphoreType.DMA((nrows,)),
            pltpu.SemaphoreType.DMA((nrows,)),
            pltpu.SemaphoreType.DMA((ncols,)),
            pltpu.SemaphoreType.DMA((ncols,)),
            pltpu.SemaphoreType.DMA((blocks,)),
            pltpu.SemaphoreType.DMA((blocks,)),
            pltpu.SemaphoreType.DMA((ncols,)),
            pltpu.SemaphoreType.DMA((ncols,)),
        ],
        compiler_params=pltpu.CompilerParams(collective_id=0, has_side_effects=True),
    )(slip_delta, block_list, live_count, kernel)


def epilogue_kernel(stress_ref, scale_ref, rate_ref, before_ref, out_ref, log_ref):
    stress = stress_ref[...]
    row = lax.broadcasted_iota(jnp.int32, stress.shape, 0)
    scale = jnp.ones_like(stress)
    rate = jnp.ones_like(stress)
    before = jnp.ones_like(stress)
    for i in range(stress.shape[0]):
        pick = row == i
        scale = jnp.where(pick, scale_ref[i], scale)
        rate = jnp.where(pick, rate_ref[i], rate)
        before = jnp.where(pick, before_ref[i], before)
    x = rate * before / scale
    u = jnp.exp(x)
    growth = jnp.where(u == 1.0, x, (u - 1.0) * x / jnp.log(u))
    out_ref[...] = stress
    log_ref[...] = jnp.log(scale / rate) + jnp.log(jnp.log1p(jnp.exp(-stress / scale) * growth))


def epilogue(stress, scale, rate, before):
    shape = jax.ShapeDtypeStruct(stress.shape, jnp.float32)
    return pl.pallas_call(
        epilogue_kernel,
        out_shape=(shape, shape),
        in_specs=[pl.BlockSpec(memory_space=pltpu.VMEM)] + [pl.BlockSpec(memory_space=pltpu.SMEM)] * 3,
        out_specs=(pl.BlockSpec(memory_space=pltpu.VMEM), pl.BlockSpec(memory_space=pltpu.VMEM)),
    )(stress, scale, rate, before)


def per_device(kernel, slip_delta, block_list, live_count, direct_effect, load_rate, time_before):
    nrows = lax.axis_size("rows")
    ncols = lax.axis_size("cols")
    stress_change = stress_sum(kernel, slip_delta, block_list, live_count, nrows, ncols)
    return epilogue(stress_change, direct_effect, load_rate, time_before)


def solution(mesh):
    in_specs = (
        P("rows", "cols"),
        P("cols", "rows", None),
        P("cols", "rows"),
        P("cols"),
        P(("rows", "cols")),
        P(("rows", "cols")),
        P(("rows", "cols")),
    )
    out_specs = (P(("rows", "cols"), None), P(("rows", "cols"), None))
    return jax.shard_map(
        per_device, mesh=mesh, in_specs=in_specs, out_specs=out_specs, check_vma=False
    )
```

```python
import functools

import jax
import jax.numpy as jnp
from jax import lax
from jax.experimental import pallas as pl
from jax.experimental.pallas import tpu as pltpu
from jax.sharding import PartitionSpec as P

BLOCK = 128
MESH = pl.DeviceIdType.MESH


def stress_kernel(nrows, ncols, groups, slip_ref, list_ref, count_ref, kernel_hbm, out_ref, pay_ref, kmat, gathered, dense_own,
                  landed, dense, sendbuf, slots, kload_sem, local_sem, g_send, g_recv, a_send, a_recv, r_send, r_recv, send_sem, recv_sem):
    me = lax.axis_index("cols")
    my_row = lax.axis_index("rows")
    share = out_ref.shape[0]
    per_group = ncols // groups
    here, list_here, patch = slip_ref.shape
    blocks = kmat.shape[1] // patch
    quarter = kmat.shape[0] // 4

    pay_ref[0] = slip_ref[...]
    for e in range(here):
        for b in range(list_here):
            live = my_row * list_here + b < count_ref[e]
            key = jnp.where(live, list_ref[e, b], -1)
            pay_ref[1, e, pl.ds(b, 1), :] = jnp.full((1, patch), key, jnp.int32).astype(jnp.float32)

    barrier = pltpu.get_barrier_semaphore()
    for k in range(1, nrows):
        peer = lax.rem(my_row + k, nrows)
        pl.semaphore_signal(barrier, inc=1, device_id=(peer, me), device_id_type=MESH)
    for k in range(1, ncols):
        peer = lax.rem(me + k, ncols)
        pl.semaphore_signal(barrier, inc=1, device_id=(my_row, peer), device_id_type=MESH)
    pl.semaphore_wait(barrier, nrows + ncols - 2)

    def entries(r):
        return pl.ds(pl.multiple_of(r * list_here, list_here), list_here)

    sends = []
    a2a_sends = []
    for k in range(1, nrows):
        peer = lax.rem(my_row + k, nrows)
        copy = pltpu.make_async_remote_copy(
            src_ref=pay_ref,
            dst_ref=gathered.at[:, :, entries(my_row)],
            send_sem=g_send.at[peer],
            recv_sem=g_recv.at[my_row],
            device_id=(peer, me),
            device_id_type=MESH,
        )
        copy.start()
        sends.append(copy)
    local = pltpu.make_async_copy(pay_ref, gathered.at[:, :, entries(my_row)], local_sem)
    local.start()
    local.wait()
    for k in range(1, nrows):
        src = lax.rem(my_row + nrows - k, nrows)
        pltpu.make_async_remote_copy(
            src_ref=pay_ref,
            dst_ref=gathered.at[:, :, entries(src)],
            send_sem=g_send.at[src],
            recv_sem=g_recv.at[src],
            device_id=(src, me),
            device_id_type=MESH,
        ).wait_recv()

    total_blocks = dense_own.shape[1]
    lane = lax.broadcasted_iota(jnp.int32, (nrows * list_here, patch), 1)
    keys = [gathered[1, e].astype(jnp.int32) for e in range(here)]
    per_piece = patch // blocks
    for q in range(total_blocks // patch):
        for e in range(here):
            onehot = (keys[e] == lane + q * patch).astype(jnp.float32)
            dense_own[e, pl.ds(q * patch, patch), :] = lax.dot_general(
                onehot,
                gathered[0, e],
                (((0,), (0,)), ((), ())),
                precision=lax.Precision.HIGHEST,
                preferred_element_type=jnp.float32,
            )
        for i in range(per_piece):
            peer = q * per_piece + i
            copy = pltpu.make_async_remote_copy(
                src_ref=dense_own.at[:, pl.ds(peer * blocks, blocks)],
                dst_ref=landed.at[pl.ds(pl.multiple_of(me * here, here), here)],
                send_sem=a_send.at[peer],
                recv_sem=a_recv.at[me],
                device_id=(my_row, peer),
                device_id_type=MESH,
            )

            @pl.when(me != peer)
            def _():
                copy.start()

            a2a_sends.append((peer, copy))

    loads = []
    for q in range(4):
        load = pltpu.make_async_copy(
            kernel_hbm.at[pl.ds(q * quarter, quarter)], kmat.at[pl.ds(q * quarter, quarter)], kload_sem.at[q]
        )
        load.start()
        loads.append(load)

    def mine(c):
        return pl.ds(pl.multiple_of(c * blocks, blocks), blocks)

    def slot(c):
        return pl.ds(pl.multiple_of(c * here, here), here)

    local = pltpu.make_async_copy(dense_own.at[:, mine(me)], landed.at[slot(me)], local_sem)
    local.start()
    local.wait()
    for k in range(1, ncols):
        src = lax.rem(me + ncols - k, ncols)
        pltpu.make_async_remote_copy(
            src_ref=dense_own.at[:, mine(src)],
            dst_ref=landed.at[slot(src)],
            send_sem=a_send.at[src],
            recv_sem=a_recv.at[src],
            device_id=(my_row, src),
            device_id_type=MESH,
        ).wait_recv()

    relayout = []
    for j in range(blocks):
        copy = pltpu.make_async_copy(landed.at[:, j], dense.at[j], r_send.at[j])
        copy.start()
        relayout.append(copy)
    for copy in relayout:
        copy.wait()
    for load in loads:
        load.wait()

    rs_sends = []
    for g in range(groups):
        rows = pl.ds(g * per_group * share, per_group * share)
        part = None
        for j in range(blocks):
            term = lax.dot_general(
                kmat[rows, pl.ds(j * patch, patch)],
                dense[j],
                (((1,), (1,)), ((), ())),
                precision=lax.Precision.HIGH,
                preferred_element_type=jnp.float32,
            )
            part = term if part is None else part + term
        for j in range(per_group):
            dest = g * per_group + j
            sendbuf[dest] = part[j * share:(j + 1) * share]
            copy = pltpu.make_async_remote_copy(
                src_ref=sendbuf.at[dest],
                dst_ref=slots.at[me],
                send_sem=send_sem.at[dest],
                recv_sem=recv_sem.at[me],
                device_id=(my_row, dest),
                device_id_type=MESH,
            )

            @pl.when(me != dest)
            def _():
                copy.start()

            rs_sends.append((dest, copy))

    total = sendbuf[me]
    for k in range(1, ncols):
        src = lax.rem(me + ncols - k, ncols)
        pltpu.make_async_remote_copy(
            src_ref=sendbuf.at[src],
            dst_ref=slots.at[src],
            send_sem=send_sem.at[src],
            recv_sem=recv_sem.at[src],
            device_id=(my_row, src),
            device_id_type=MESH,
        ).wait_recv()
        total = total + slots[src]
    out_ref[...] = total
    for copy in sends:
        copy.wait_send()
    for dest, copy in a2a_sends + rs_sends:

        @pl.when(me != dest)
        def _():
            copy.wait_send()


def stress_sum(kernel, slip_delta, block_list, live_count, nrows, ncols, groups=16):
    rows, sources = kernel.shape
    here, list_here, patch = slip_delta.shape
    events = ncols * here
    share = rows // ncols
    blocks = sources // patch
    return pl.pallas_call(
        functools.partial(stress_kernel, nrows, ncols, groups),
        out_shape=jax.ShapeDtypeStruct((share, events), jnp.float32),
        in_specs=[
            pl.BlockSpec(memory_space=pltpu.VMEM),
            pl.BlockSpec(memory_space=pltpu.SMEM),
            pl.BlockSpec(memory_space=pltpu.SMEM),
            pl.BlockSpec(memory_space=pl.ANY),
        ],
        out_specs=pl.BlockSpec(memory_space=pltpu.VMEM),
        scratch_shapes=[
            pltpu.VMEM((2, here, list_here, patch), jnp.float32),
            pltpu.VMEM((rows, sources), jnp.float32),
            pltpu.VMEM((2, here, nrows * list_here, patch), jnp.float32),
            pltpu.VMEM((here, ncols * blocks, patch), jnp.float32),
            pltpu.VMEM((events, blocks, patch), jnp.float32),
            pltpu.VMEM((blocks, events, patch), jnp.float32),
            pltpu.VMEM((ncols, share, events), jnp.float32),
            pltpu.VMEM((ncols, share, events), jnp.float32),
            pltpu.SemaphoreType.DMA((4,)),
            pltpu.SemaphoreType.DMA,
            pltpu.SemaphoreType.DMA((nrows,)),
            pltpu.SemaphoreType.DMA((nrows,)),
            pltpu.SemaphoreType.DMA((ncols,)),
            pltpu.SemaphoreType.DMA((ncols,)),
            pltpu.SemaphoreType.DMA((blocks,)),
            pltpu.SemaphoreType.DMA((blocks,)),
            pltpu.SemaphoreType.DMA((ncols,)),
            pltpu.SemaphoreType.DMA((ncols,)),
        ],
        compiler_params=pltpu.CompilerParams(collective_id=0, has_side_effects=True),
    )(slip_delta, block_list, live_count, kernel)


def epilogue_kernel(stress_ref, scale_ref, rate_ref, before_ref, out_ref, log_ref):
    stress = stress_ref[...]
    row = lax.broadcasted_iota(jnp.int32, stress.shape, 0)
    scale = jnp.ones_like(stress)
    rate = jnp.ones_like(stress)
    before = jnp.ones_like(stress)
    for i in range(stress.shape[0]):
        pick = row == i
        scale = jnp.where(pick, scale_ref[i], scale)
        rate = jnp.where(pick, rate_ref[i], rate)
        before = jnp.where(pick, before_ref[i], before)
    x = rate * before / scale
    u = jnp.exp(x)
    growth = jnp.where(u == 1.0, x, (u - 1.0) * x / jnp.log(u))
    out_ref[...] = stress
    log_ref[...] = jnp.log(scale / rate) + jnp.log(jnp.log1p(jnp.exp(-stress / scale) * growth))


def epilogue(stress, scale, rate, before):
    shape = jax.ShapeDtypeStruct(stress.shape, jnp.float32)
    return pl.pallas_call(
        epilogue_kernel,
        out_shape=(shape, shape),
        in_specs=[pl.BlockSpec(memory_space=pltpu.VMEM)] + [pl.BlockSpec(memory_space=pltpu.SMEM)] * 3,
        out_specs=(pl.BlockSpec(memory_space=pltpu.VMEM), pl.BlockSpec(memory_space=pltpu.VMEM)),
    )(stress, scale, rate, before)


def per_device(kernel, slip_delta, block_list, live_count, direct_effect, load_rate, time_before):
    nrows = lax.axis_size("rows")
    ncols = lax.axis_size("cols")
    stress_change = stress_sum(kernel, slip_delta, block_list, live_count, nrows, ncols)
    return epilogue(stress_change, direct_effect, load_rate, time_before)


def solution(mesh):
    in_specs = (
        P("rows", "cols"),
        P("cols", "rows", None),
        P("cols", "rows"),
        P("cols"),
        P(("rows", "cols")),
        P(("rows", "cols")),
        P(("rows", "cols")),
    )
    out_specs = (P(("rows", "cols"), None), P(("rows", "cols"), None))
    return jax.shard_map(
        per_device, mesh=mesh, in_specs=in_specs, out_specs=out_specs, check_vma=False
    )
```

```python
import functools

import jax
import jax.numpy as jnp
from jax import lax
from jax.experimental import pallas as pl
from jax.experimental.pallas import tpu as pltpu
from jax.sharding import PartitionSpec as P

BLOCK = 128
MESH = pl.DeviceIdType.MESH


def stress_kernel(nrows, ncols, groups, slip_ref, list_ref, count_ref, kernel_hbm, out_ref, pay_ref, kmat, gathered, dense_own,
                  landed, dense, sendbuf, slots, kload_sem, local_sem, g_send, g_recv, a_send, a_recv, r_send, r_recv, send_sem, recv_sem):
    me = lax.axis_index("cols")
    my_row = lax.axis_index("rows")
    share = out_ref.shape[0]
    per_group = ncols // groups
    here, list_here, patch = slip_ref.shape
    blocks = kmat.shape[1] // patch
    quarter = kmat.shape[0] // 4

    pay_ref[0] = slip_ref[...]
    for e in range(here):
        for b in range(list_here):
            live = my_row * list_here + b < count_ref[e]
            key = jnp.where(live, list_ref[e, b], -1)
            pay_ref[1, e, pl.ds(b, 1), :] = jnp.full((1, patch), key, jnp.int32).astype(jnp.float32)

    barrier = pltpu.get_barrier_semaphore()
    for k in range(1, nrows):
        peer = lax.rem(my_row + k, nrows)
        pl.semaphore_signal(barrier, inc=1, device_id=(peer, me), device_id_type=MESH)
    for k in range(1, ncols):
        peer = lax.rem(me + k, ncols)
        pl.semaphore_signal(barrier, inc=1, device_id=(my_row, peer), device_id_type=MESH)
    pl.semaphore_wait(barrier, nrows + ncols - 2)

    def entries(r):
        return pl.ds(pl.multiple_of(r * list_here, list_here), list_here)

    sends = []
    a2a_sends = []
    for k in range(1, nrows):
        peer = lax.rem(my_row + k, nrows)
        copy = pltpu.make_async_remote_copy(
            src_ref=pay_ref,
            dst_ref=gathered.at[:, :, entries(my_row)],
            send_sem=g_send.at[peer],
            recv_sem=g_recv.at[my_row],
            device_id=(peer, me),
            device_id_type=MESH,
        )
        copy.start()
        sends.append(copy)
    local = pltpu.make_async_copy(pay_ref, gathered.at[:, :, entries(my_row)], local_sem)
    local.start()
    local.wait()
    for k in range(1, nrows):
        src = lax.rem(my_row + nrows - k, nrows)
        pltpu.make_async_remote_copy(
            src_ref=pay_ref,
            dst_ref=gathered.at[:, :, entries(src)],
            send_sem=g_send.at[src],
            recv_sem=g_recv.at[src],
            device_id=(src, me),
            device_id_type=MESH,
        ).wait_recv()

    total_blocks = dense_own.shape[1]
    lane = lax.broadcasted_iota(jnp.int32, (nrows * list_here, patch), 1)
    keys = [gathered[1, e].astype(jnp.int32) for e in range(here)]
    parts = []
    for e in range(here):
        slip = gathered[0, e]
        hi = slip.astype(jnp.bfloat16)
        rest = slip - hi.astype(jnp.float32)
        mid = rest.astype(jnp.bfloat16)
        lo = (rest - mid.astype(jnp.float32)).astype(jnp.bfloat16)
        parts.append((hi, mid, lo))
    per_piece = patch // blocks
    for q in range(total_blocks // patch):
        for e in range(here):
            onehot = (keys[e] == lane + q * patch).astype(jnp.bfloat16)
            terms = [
                lax.dot_general(
                    onehot, part, (((0,), (0,)), ((), ())), preferred_element_type=jnp.float32
                )
                for part in parts[e]
            ]
            dense_own[e, pl.ds(q * patch, patch), :] = (terms[0] + terms[1]) + terms[2]
        for i in range(per_piece):
            peer = q * per_piece + i
            copy = pltpu.make_async_remote_copy(
                src_ref=dense_own.at[:, pl.ds(peer * blocks, blocks)],
                dst_ref=landed.at[pl.ds(pl.multiple_of(me * here, here), here)],
                send_sem=a_send.at[peer],
                recv_sem=a_recv.at[me],
                device_id=(my_row, peer),
                device_id_type=MESH,
            )

            @pl.when(me != peer)
            def _():
                copy.start()

            a2a_sends.append((peer, copy))

    loads = []
    for q in range(4):
        load = pltpu.make_async_copy(
            kernel_hbm.at[pl.ds(q * quarter, quarter)], kmat.at[pl.ds(q * quarter, quarter)], kload_sem.at[q]
        )
        load.start()
        loads.append(load)

    def mine(c):
        return pl.ds(pl.multiple_of(c * blocks, blocks), blocks)

    def slot(c):
        return pl.ds(pl.multiple_of(c * here, here), here)

    local = pltpu.make_async_copy(dense_own.at[:, mine(me)], landed.at[slot(me)], local_sem)
    local.start()
    local.wait()
    for k in range(1, ncols):
        src = lax.rem(me + ncols - k, ncols)
        pltpu.make_async_remote_copy(
            src_ref=dense_own.at[:, mine(src)],
            dst_ref=landed.at[slot(src)],
            send_sem=a_send.at[src],
            recv_sem=a_recv.at[src],
            device_id=(my_row, src),
            device_id_type=MESH,
        ).wait_recv()

    relayout = []
    for j in range(blocks):
        copy = pltpu.make_async_copy(landed.at[:, j], dense.at[j], r_send.at[j])
        copy.start()
        relayout.append(copy)
    for load in loads:
        load.wait()

    rs_sends = []
    for g in range(groups):
        rows = pl.ds(g * per_group * share, per_group * share)
        part = None
        for j in range(blocks):
            if g == 0:
                relayout[j].wait()
            term = lax.dot_general(
                kmat[rows, pl.ds(j * patch, patch)],
                dense[j],
                (((1,), (1,)), ((), ())),
                precision=lax.Precision.HIGH,
                preferred_element_type=jnp.float32,
            )
            part = term if part is None else part + term
        for j in range(per_group):
            dest = g * per_group + j
            sendbuf[dest] = part[j * share:(j + 1) * share]
            copy = pltpu.make_async_remote_copy(
                src_ref=sendbuf.at[dest],
                dst_ref=slots.at[me],
                send_sem=send_sem.at[dest],
                recv_sem=recv_sem.at[me],
                device_id=(my_row, dest),
                device_id_type=MESH,
            )

            @pl.when(me != dest)
            def _():
                copy.start()

            rs_sends.append((dest, copy))

    total = sendbuf[me]
    for k in range(1, ncols):
        src = lax.rem(me + ncols - k, ncols)
        pltpu.make_async_remote_copy(
            src_ref=sendbuf.at[src],
            dst_ref=slots.at[src],
            send_sem=send_sem.at[src],
            recv_sem=recv_sem.at[src],
            device_id=(my_row, src),
            device_id_type=MESH,
        ).wait_recv()
        total = total + slots[src]
    out_ref[...] = total
    for copy in sends:
        copy.wait_send()
    for dest, copy in a2a_sends + rs_sends:

        @pl.when(me != dest)
        def _():
            copy.wait_send()


def stress_sum(kernel, slip_delta, block_list, live_count, nrows, ncols, groups=8):
    rows, sources = kernel.shape
    here, list_here, patch = slip_delta.shape
    events = ncols * here
    share = rows // ncols
    blocks = sources // patch
    return pl.pallas_call(
        functools.partial(stress_kernel, nrows, ncols, groups),
        out_shape=jax.ShapeDtypeStruct((share, events), jnp.float32),
        in_specs=[
            pl.BlockSpec(memory_space=pltpu.VMEM),
            pl.BlockSpec(memory_space=pltpu.SMEM),
            pl.BlockSpec(memory_space=pltpu.SMEM),
            pl.BlockSpec(memory_space=pl.ANY),
        ],
        out_specs=pl.BlockSpec(memory_space=pltpu.VMEM),
        scratch_shapes=[
            pltpu.VMEM((2, here, list_here, patch), jnp.float32),
            pltpu.VMEM((rows, sources), jnp.float32),
            pltpu.VMEM((2, here, nrows * list_here, patch), jnp.float32),
            pltpu.VMEM((here, ncols * blocks, patch), jnp.float32),
            pltpu.VMEM((events, blocks, patch), jnp.float32),
            pltpu.VMEM((blocks, events, patch), jnp.float32),
            pltpu.VMEM((ncols, share, events), jnp.float32),
            pltpu.VMEM((ncols, share, events), jnp.float32),
            pltpu.SemaphoreType.DMA((4,)),
            pltpu.SemaphoreType.DMA,
            pltpu.SemaphoreType.DMA((nrows,)),
            pltpu.SemaphoreType.DMA((nrows,)),
            pltpu.SemaphoreType.DMA((ncols,)),
            pltpu.SemaphoreType.DMA((ncols,)),
            pltpu.SemaphoreType.DMA((blocks,)),
            pltpu.SemaphoreType.DMA((blocks,)),
            pltpu.SemaphoreType.DMA((ncols,)),
            pltpu.SemaphoreType.DMA((ncols,)),
        ],
        compiler_params=pltpu.CompilerParams(collective_id=0, has_side_effects=True),
    )(slip_delta, block_list, live_count, kernel)


def epilogue_kernel(stress_ref, scale_ref, rate_ref, before_ref, out_ref, log_ref):
    stress = stress_ref[...]
    row = lax.broadcasted_iota(jnp.int32, stress.shape, 0)
    scale = jnp.ones_like(stress)
    rate = jnp.ones_like(stress)
    before = jnp.ones_like(stress)
    for i in range(stress.shape[0]):
        pick = row == i
        scale = jnp.where(pick, scale_ref[i], scale)
        rate = jnp.where(pick, rate_ref[i], rate)
        before = jnp.where(pick, before_ref[i], before)
    x = rate * before / scale
    u = jnp.exp(x)
    growth = jnp.where(u == 1.0, x, (u - 1.0) * x / jnp.log(u))
    out_ref[...] = stress
    log_ref[...] = jnp.log(scale / rate) + jnp.log(jnp.log1p(jnp.exp(-stress / scale) * growth))


def epilogue(stress, scale, rate, before):
    shape = jax.ShapeDtypeStruct(stress.shape, jnp.float32)
    return pl.pallas_call(
        epilogue_kernel,
        out_shape=(shape, shape),
        in_specs=[pl.BlockSpec(memory_space=pltpu.VMEM)] + [pl.BlockSpec(memory_space=pltpu.SMEM)] * 3,
        out_specs=(pl.BlockSpec(memory_space=pltpu.VMEM), pl.BlockSpec(memory_space=pltpu.VMEM)),
    )(stress, scale, rate, before)


def per_device(kernel, slip_delta, block_list, live_count, direct_effect, load_rate, time_before):
    nrows = lax.axis_size("rows")
    ncols = lax.axis_size("cols")
    stress_change = stress_sum(kernel, slip_delta, block_list, live_count, nrows, ncols)
    return epilogue(stress_change, direct_effect, load_rate, time_before)


def solution(mesh):
    in_specs = (
        P("rows", "cols"),
        P("cols", "rows", None),
        P("cols", "rows"),
        P("cols"),
        P(("rows", "cols")),
        P(("rows", "cols")),
        P(("rows", "cols")),
    )
    out_specs = (P(("rows", "cols"), None), P(("rows", "cols"), None))
    return jax.shard_map(
        per_device, mesh=mesh, in_specs=in_specs, out_specs=out_specs, check_vma=False
    )
```

```python
import functools

import jax
import jax.numpy as jnp
from jax import lax
from jax.experimental import pallas as pl
from jax.experimental.pallas import tpu as pltpu
from jax.sharding import PartitionSpec as P

BLOCK = 128
MESH = pl.DeviceIdType.MESH


def stress_kernel(nrows, ncols, groups, slip_ref, list_ref, count_ref, kernel_hbm, out_ref, pay_ref, kmat, gathered, dense_own,
                  landed, dense, sendbuf, slots, kload_sem, local_sem, g_send, g_recv, a_send, a_recv, r_send, r_recv, send_sem, recv_sem):
    me = lax.axis_index("cols")
    my_row = lax.axis_index("rows")
    share = out_ref.shape[0]
    per_group = ncols // groups
    here, list_here, patch = slip_ref.shape
    blocks = kmat.shape[1] // patch
    quarter = kmat.shape[0] // 4

    pay_ref[0] = slip_ref[...]
    for e in range(here):
        for b in range(list_here):
            live = my_row * list_here + b < count_ref[e]
            key = jnp.where(live, list_ref[e, b], -1)
            pay_ref[1, e, pl.ds(b, 1), :] = jnp.full((1, patch), key, jnp.int32).astype(jnp.float32)

    barrier = pltpu.get_barrier_semaphore()
    for k in range(1, nrows):
        peer = lax.rem(my_row + k, nrows)
        pl.semaphore_signal(barrier, inc=1, device_id=(peer, me), device_id_type=MESH)
    for k in range(1, ncols):
        peer = lax.rem(me + k, ncols)
        pl.semaphore_signal(barrier, inc=1, device_id=(my_row, peer), device_id_type=MESH)
    pl.semaphore_wait(barrier, nrows + ncols - 2)

    def entries(r):
        return pl.ds(pl.multiple_of(r * list_here, list_here), list_here)

    sends = []
    a2a_sends = []
    for k in range(1, nrows):
        peer = lax.rem(my_row + k, nrows)
        copy = pltpu.make_async_remote_copy(
            src_ref=pay_ref,
            dst_ref=gathered.at[:, :, entries(my_row)],
            send_sem=g_send.at[peer],
            recv_sem=g_recv.at[my_row],
            device_id=(peer, me),
            device_id_type=MESH,
        )
        copy.start()
        sends.append(copy)
    local = pltpu.make_async_copy(pay_ref, gathered.at[:, :, entries(my_row)], local_sem)
    local.start()
    local.wait()
    for k in range(1, nrows):
        src = lax.rem(my_row + nrows - k, nrows)
        pltpu.make_async_remote_copy(
            src_ref=pay_ref,
            dst_ref=gathered.at[:, :, entries(src)],
            send_sem=g_send.at[src],
            recv_sem=g_recv.at[src],
            device_id=(src, me),
            device_id_type=MESH,
        ).wait_recv()

    total_blocks = dense_own.shape[1]
    lane = lax.broadcasted_iota(jnp.int32, (nrows * list_here, patch), 1)
    keys = [gathered[1, e].astype(jnp.int32) for e in range(here)]
    parts = []
    for e in range(here):
        slip = gathered[0, e]
        hi = slip.astype(jnp.bfloat16)
        rest = slip - hi.astype(jnp.float32)
        mid = rest.astype(jnp.bfloat16)
        lo = (rest - mid.astype(jnp.float32)).astype(jnp.bfloat16)
        parts.append((hi, mid, lo))
    per_piece = patch // blocks
    pieces = total_blocks // patch
    for q in range(pieces):
        qq = lax.rem(q + me // per_piece + 1, pieces)
        for e in range(here):
            onehot = (keys[e] == lane + qq * patch).astype(jnp.bfloat16)
            terms = [
                lax.dot_general(
                    onehot, part, (((0,), (0,)), ((), ())), preferred_element_type=jnp.float32
                )
                for part in parts[e]
            ]
            dense_own[e, pl.ds(pl.multiple_of(qq * patch, patch), patch), :] = (terms[0] + terms[1]) + terms[2]
        for i in range(per_piece):
            peer = qq * per_piece + lax.rem(i + me, per_piece)
            copy = pltpu.make_async_remote_copy(
                src_ref=dense_own.at[:, pl.ds(pl.multiple_of(peer * blocks, blocks), blocks)],
                dst_ref=landed.at[pl.ds(pl.multiple_of(me * here, here), here)],
                send_sem=a_send.at[peer],
                recv_sem=a_recv.at[me],
                device_id=(my_row, peer),
                device_id_type=MESH,
            )

            @pl.when(me != peer)
            def _():
                copy.start()

            a2a_sends.append((peer, copy))

    loads = []
    for q in range(4):
        load = pltpu.make_async_copy(
            kernel_hbm.at[pl.ds(q * quarter, quarter)], kmat.at[pl.ds(q * quarter, quarter)], kload_sem.at[q]
        )
        load.start()
        loads.append(load)

    def mine(c):
        return pl.ds(pl.multiple_of(c * blocks, blocks), blocks)

    def slot(c):
        return pl.ds(pl.multiple_of(c * here, here), here)

    local = pltpu.make_async_copy(dense_own.at[:, mine(me)], landed.at[slot(me)], local_sem)
    local.start()
    local.wait()
    for k in range(1, ncols):
        src = lax.rem(me + ncols - k, ncols)
        pltpu.make_async_remote_copy(
            src_ref=dense_own.at[:, mine(src)],
            dst_ref=landed.at[slot(src)],
            send_sem=a_send.at[src],
            recv_sem=a_recv.at[src],
            device_id=(my_row, src),
            device_id_type=MESH,
        ).wait_recv()

    relayout = []
    for j in range(blocks):
        copy = pltpu.make_async_copy(landed.at[:, j], dense.at[j], r_send.at[j])
        copy.start()
        relayout.append(copy)
    for load in loads:
        load.wait()

    rs_sends = []
    for g in range(groups):
        gg = lax.rem(g + me // per_group + 1, groups)
        rows = pl.ds(pl.multiple_of(gg * per_group * share, per_group * share), per_group * share)
        part = None
        for j in range(blocks):
            if g == 0:
                relayout[j].wait()
            term = lax.dot_general(
                kmat[rows, pl.ds(j * patch, patch)],
                dense[j],
                (((1,), (1,)), ((), ())),
                precision=lax.Precision.HIGH,
                preferred_element_type=jnp.float32,
            )
            part = term if part is None else part + term
        for j in range(per_group):
            sendbuf[gg * per_group + j] = part[j * share:(j + 1) * share]
        for j in range(per_group):
            dest = gg * per_group + lax.rem(j + me, per_group)
            copy = pltpu.make_async_remote_copy(
                src_ref=sendbuf.at[dest],
                dst_ref=slots.at[me],
                send_sem=send_sem.at[dest],
                recv_sem=recv_sem.at[me],
                device_id=(my_row, dest),
                device_id_type=MESH,
            )

            @pl.when(me != dest)
            def _():
                copy.start()

            rs_sends.append((dest, copy))

    total = sendbuf[me]
    for k in range(1, ncols):
        src = lax.rem(me + ncols - k, ncols)
        pltpu.make_async_remote_copy(
            src_ref=sendbuf.at[src],
            dst_ref=slots.at[src],
            send_sem=send_sem.at[src],
            recv_sem=recv_sem.at[src],
            device_id=(my_row, src),
            device_id_type=MESH,
        ).wait_recv()
        total = total + slots[src]
    out_ref[...] = total
    for copy in sends:
        copy.wait_send()
    for dest, copy in a2a_sends + rs_sends:

        @pl.when(me != dest)
        def _():
            copy.wait_send()


def stress_sum(kernel, slip_delta, block_list, live_count, nrows, ncols, groups=8):
    rows, sources = kernel.shape
    here, list_here, patch = slip_delta.shape
    events = ncols * here
    share = rows // ncols
    blocks = sources // patch
    return pl.pallas_call(
        functools.partial(stress_kernel, nrows, ncols, groups),
        out_shape=jax.ShapeDtypeStruct((share, events), jnp.float32),
        in_specs=[
            pl.BlockSpec(memory_space=pltpu.VMEM),
            pl.BlockSpec(memory_space=pltpu.SMEM),
            pl.BlockSpec(memory_space=pltpu.SMEM),
            pl.BlockSpec(memory_space=pl.ANY),
        ],
        out_specs=pl.BlockSpec(memory_space=pltpu.VMEM),
        scratch_shapes=[
            pltpu.VMEM((2, here, list_here, patch), jnp.float32),
            pltpu.VMEM((rows, sources), jnp.float32),
            pltpu.VMEM((2, here, nrows * list_here, patch), jnp.float32),
            pltpu.VMEM((here, ncols * blocks, patch), jnp.float32),
            pltpu.VMEM((events, blocks, patch), jnp.float32),
            pltpu.VMEM((blocks, events, patch), jnp.float32),
            pltpu.VMEM((ncols, share, events), jnp.float32),
            pltpu.VMEM((ncols, share, events), jnp.float32),
            pltpu.SemaphoreType.DMA((4,)),
            pltpu.SemaphoreType.DMA,
            pltpu.SemaphoreType.DMA((nrows,)),
            pltpu.SemaphoreType.DMA((nrows,)),
            pltpu.SemaphoreType.DMA((ncols,)),
            pltpu.SemaphoreType.DMA((ncols,)),
            pltpu.SemaphoreType.DMA((blocks,)),
            pltpu.SemaphoreType.DMA((blocks,)),
            pltpu.SemaphoreType.DMA((ncols,)),
            pltpu.SemaphoreType.DMA((ncols,)),
        ],
        compiler_params=pltpu.CompilerParams(collective_id=0, has_side_effects=True),
    )(slip_delta, block_list, live_count, kernel)


def epilogue_kernel(stress_ref, scale_ref, rate_ref, before_ref, out_ref, log_ref):
    stress = stress_ref[...]
    row = lax.broadcasted_iota(jnp.int32, stress.shape, 0)
    scale = jnp.ones_like(stress)
    rate = jnp.ones_like(stress)
    before = jnp.ones_like(stress)
    for i in range(stress.shape[0]):
        pick = row == i
        scale = jnp.where(pick, scale_ref[i], scale)
        rate = jnp.where(pick, rate_ref[i], rate)
        before = jnp.where(pick, before_ref[i], before)
    x = rate * before / scale
    u = jnp.exp(x)
    growth = jnp.where(u == 1.0, x, (u - 1.0) * x / jnp.log(u))
    out_ref[...] = stress
    log_ref[...] = jnp.log(scale / rate) + jnp.log(jnp.log1p(jnp.exp(-stress / scale) * growth))


def epilogue(stress, scale, rate, before):
    shape = jax.ShapeDtypeStruct(stress.shape, jnp.float32)
    return pl.pallas_call(
        epilogue_kernel,
        out_shape=(shape, shape),
        in_specs=[pl.BlockSpec(memory_space=pltpu.VMEM)] + [pl.BlockSpec(memory_space=pltpu.SMEM)] * 3,
        out_specs=(pl.BlockSpec(memory_space=pltpu.VMEM), pl.BlockSpec(memory_space=pltpu.VMEM)),
    )(stress, scale, rate, before)


def per_device(kernel, slip_delta, block_list, live_count, direct_effect, load_rate, time_before):
    nrows = lax.axis_size("rows")
    ncols = lax.axis_size("cols")
    stress_change = stress_sum(kernel, slip_delta, block_list, live_count, nrows, ncols)
    return epilogue(stress_change, direct_effect, load_rate, time_before)


def solution(mesh):
    in_specs = (
        P("rows", "cols"),
        P("cols", "rows", None),
        P("cols", "rows"),
        P("cols"),
        P(("rows", "cols")),
        P(("rows", "cols")),
        P(("rows", "cols")),
    )
    out_specs = (P(("rows", "cols"), None), P(("rows", "cols"), None))
    return jax.shard_map(
        per_device, mesh=mesh, in_specs=in_specs, out_specs=out_specs, check_vma=False
    )
```

```python
import functools

import jax
import jax.numpy as jnp
from jax import lax
from jax.experimental import pallas as pl
from jax.experimental.pallas import tpu as pltpu
from jax.sharding import PartitionSpec as P

BLOCK = 128
MESH = pl.DeviceIdType.MESH


def stress_kernel(nrows, ncols, groups, slip_ref, list_ref, count_ref, kernel_hbm, out_ref, pay_ref, kmat, gathered, dense_own,
                  landed, dense, sendbuf, slots, kload_sem, local_sem, g_send, g_recv, a_send, a_recv, r_send, r_recv, send_sem, recv_sem):
    me = lax.axis_index("cols")
    my_row = lax.axis_index("rows")
    share = out_ref.shape[0]
    per_group = ncols // groups
    here, list_here, patch = slip_ref.shape
    blocks = kmat.shape[1] // patch
    quarter = kmat.shape[0] // 4

    pay_ref[0] = slip_ref[...]
    for e in range(here):
        for b in range(list_here):
            live = my_row * list_here + b < count_ref[e]
            key = jnp.where(live, list_ref[e, b], -1)
            pay_ref[1, e, pl.ds(b, 1), :] = jnp.full((1, patch), key, jnp.int32).astype(jnp.float32)

    barrier = pltpu.get_barrier_semaphore()
    for k in range(1, nrows):
        peer = lax.rem(my_row + k, nrows)
        pl.semaphore_signal(barrier, inc=1, device_id=(peer, me), device_id_type=MESH)
    for k in range(1, ncols):
        peer = lax.rem(me + k, ncols)
        pl.semaphore_signal(barrier, inc=1, device_id=(my_row, peer), device_id_type=MESH)
    pl.semaphore_wait(barrier, nrows + ncols - 2)

    def entries(r):
        return pl.ds(pl.multiple_of(r * list_here, list_here), list_here)

    sends = []
    a2a_sends = []
    for k in range(1, nrows):
        peer = lax.rem(my_row + k, nrows)
        copy = pltpu.make_async_remote_copy(
            src_ref=pay_ref,
            dst_ref=gathered.at[:, :, entries(my_row)],
            send_sem=g_send.at[peer],
            recv_sem=g_recv.at[my_row],
            device_id=(peer, me),
            device_id_type=MESH,
        )
        copy.start()
        sends.append(copy)
    local = pltpu.make_async_copy(pay_ref, gathered.at[:, :, entries(my_row)], local_sem)
    local.start()
    local.wait()
    for k in range(1, nrows):
        src = lax.rem(my_row + nrows - k, nrows)
        pltpu.make_async_remote_copy(
            src_ref=pay_ref,
            dst_ref=gathered.at[:, :, entries(src)],
            send_sem=g_send.at[src],
            recv_sem=g_recv.at[src],
            device_id=(src, me),
            device_id_type=MESH,
        ).wait_recv()

    total_blocks = dense_own.shape[1]
    lane = lax.broadcasted_iota(jnp.int32, (nrows * list_here, patch), 1)
    keys = [gathered[1, e].astype(jnp.int32) for e in range(here)]
    per_piece = patch // blocks
    for q in range(total_blocks // patch):
        for e in range(here):
            onehot = (keys[e] == lane + q * patch).astype(jnp.float32)
            dense_own[e, pl.ds(q * patch, patch), :] = lax.dot_general(
                onehot,
                gathered[0, e],
                (((0,), (0,)), ((), ())),
                precision=lax.Precision.HIGHEST,
                preferred_element_type=jnp.float32,
            )
        for i in range(per_piece):
            peer = q * per_piece + i
            copy = pltpu.make_async_remote_copy(
                src_ref=dense_own.at[:, pl.ds(peer * blocks, blocks)],
                dst_ref=landed.at[pl.ds(pl.multiple_of(me * here, here), here)],
                send_sem=a_send.at[peer],
                recv_sem=a_recv.at[me],
                device_id=(my_row, peer),
                device_id_type=MESH,
            )

            @pl.when(me != peer)
            def _():
                copy.start()

            a2a_sends.append((peer, copy))

    loads = []
    for q in range(4):
        load = pltpu.make_async_copy(
            kernel_hbm.at[pl.ds(q * quarter, quarter)], kmat.at[pl.ds(q * quarter, quarter)], kload_sem.at[q]
        )
        load.start()
        loads.append(load)

    def mine(c):
        return pl.ds(pl.multiple_of(c * blocks, blocks), blocks)

    def slot(c):
        return pl.ds(pl.multiple_of(c * here, here), here)

    local = pltpu.make_async_copy(dense_own.at[:, mine(me)], landed.at[slot(me)], local_sem)
    local.start()
    local.wait()
    for k in range(1, ncols):
        src = lax.rem(me + ncols - k, ncols)
        pltpu.make_async_remote_copy(
            src_ref=dense_own.at[:, mine(src)],
            dst_ref=landed.at[slot(src)],
            send_sem=a_send.at[src],
            recv_sem=a_recv.at[src],
            device_id=(my_row, src),
            device_id_type=MESH,
        ).wait_recv()

    relayout = []
    for j in range(blocks):
        copy = pltpu.make_async_copy(landed.at[:, j], dense.at[j], r_send.at[j])
        copy.start()
        relayout.append(copy)
    for copy in relayout:
        copy.wait()
    for load in loads:
        load.wait()

    rs_sends = []
    for g in range(groups):
        gg = lax.rem(g + me // per_group + 1, groups)
        rows = pl.ds(pl.multiple_of(gg * per_group * share, per_group * share), per_group * share)
        part = None
        for j in range(blocks):
            term = lax.dot_general(
                kmat[rows, pl.ds(j * patch, patch)],
                dense[j],
                (((1,), (1,)), ((), ())),
                precision=lax.Precision.HIGH,
                preferred_element_type=jnp.float32,
            )
            part = term if part is None else part + term
        for j in range(per_group):
            dest = gg * per_group + j
            sendbuf[dest] = part[j * share:(j + 1) * share]
            copy = pltpu.make_async_remote_copy(
                src_ref=sendbuf.at[dest],
                dst_ref=slots.at[me],
                send_sem=send_sem.at[dest],
                recv_sem=recv_sem.at[me],
                device_id=(my_row, dest),
                device_id_type=MESH,
            )

            @pl.when(me != dest)
            def _():
                copy.start()

            rs_sends.append((dest, copy))

    total = sendbuf[me]
    for k in range(1, ncols):
        src = lax.rem(me + ncols - k, ncols)
        pltpu.make_async_remote_copy(
            src_ref=sendbuf.at[src],
            dst_ref=slots.at[src],
            send_sem=send_sem.at[src],
            recv_sem=recv_sem.at[src],
            device_id=(my_row, src),
            device_id_type=MESH,
        ).wait_recv()
        total = total + slots[src]
    out_ref[...] = total
    for copy in sends:
        copy.wait_send()
    for dest, copy in a2a_sends + rs_sends:

        @pl.when(me != dest)
        def _():
            copy.wait_send()


def stress_sum(kernel, slip_delta, block_list, live_count, nrows, ncols, groups=8):
    rows, sources = kernel.shape
    here, list_here, patch = slip_delta.shape
    events = ncols * here
    share = rows // ncols
    blocks = sources // patch
    return pl.pallas_call(
        functools.partial(stress_kernel, nrows, ncols, groups),
        out_shape=jax.ShapeDtypeStruct((share, events), jnp.float32),
        in_specs=[
            pl.BlockSpec(memory_space=pltpu.VMEM),
            pl.BlockSpec(memory_space=pltpu.SMEM),
            pl.BlockSpec(memory_space=pltpu.SMEM),
            pl.BlockSpec(memory_space=pl.ANY),
        ],
        out_specs=pl.BlockSpec(memory_space=pltpu.VMEM),
        scratch_shapes=[
            pltpu.VMEM((2, here, list_here, patch), jnp.float32),
            pltpu.VMEM((rows, sources), jnp.float32),
            pltpu.VMEM((2, here, nrows * list_here, patch), jnp.float32),
            pltpu.VMEM((here, ncols * blocks, patch), jnp.float32),
            pltpu.VMEM((events, blocks, patch), jnp.float32),
            pltpu.VMEM((blocks, events, patch), jnp.float32),
            pltpu.VMEM((ncols, share, events), jnp.float32),
            pltpu.VMEM((ncols, share, events), jnp.float32),
            pltpu.SemaphoreType.DMA((4,)),
            pltpu.SemaphoreType.DMA,
            pltpu.SemaphoreType.DMA((nrows,)),
            pltpu.SemaphoreType.DMA((nrows,)),
            pltpu.SemaphoreType.DMA((ncols,)),
            pltpu.SemaphoreType.DMA((ncols,)),
            pltpu.SemaphoreType.DMA((blocks,)),
            pltpu.SemaphoreType.DMA((blocks,)),
            pltpu.SemaphoreType.DMA((ncols,)),
            pltpu.SemaphoreType.DMA((ncols,)),
        ],
        compiler_params=pltpu.CompilerParams(collective_id=0, has_side_effects=True),
    )(slip_delta, block_list, live_count, kernel)


def epilogue_kernel(stress_ref, scale_ref, rate_ref, before_ref, out_ref, log_ref):
    stress = stress_ref[...]
    row = lax.broadcasted_iota(jnp.int32, stress.shape, 0)
    scale = jnp.ones_like(stress)
    rate = jnp.ones_like(stress)
    before = jnp.ones_like(stress)
    for i in range(stress.shape[0]):
        pick = row == i
        scale = jnp.where(pick, scale_ref[i], scale)
        rate = jnp.where(pick, rate_ref[i], rate)
        before = jnp.where(pick, before_ref[i], before)
    x = rate * before / scale
    u = jnp.exp(x)
    growth = jnp.where(u == 1.0, x, (u - 1.0) * x / jnp.log(u))
    out_ref[...] = stress
    log_ref[...] = jnp.log(scale / rate) + jnp.log(jnp.log1p(jnp.exp(-stress / scale) * growth))


def epilogue(stress, scale, rate, before):
    shape = jax.ShapeDtypeStruct(stress.shape, jnp.float32)
    return pl.pallas_call(
        epilogue_kernel,
        out_shape=(shape, shape),
        in_specs=[pl.BlockSpec(memory_space=pltpu.VMEM)] + [pl.BlockSpec(memory_space=pltpu.SMEM)] * 3,
        out_specs=(pl.BlockSpec(memory_space=pltpu.VMEM), pl.BlockSpec(memory_space=pltpu.VMEM)),
    )(stress, scale, rate, before)


def per_device(kernel, slip_delta, block_list, live_count, direct_effect, load_rate, time_before):
    nrows = lax.axis_size("rows")
    ncols = lax.axis_size("cols")
    stress_change = stress_sum(kernel, slip_delta, block_list, live_count, nrows, ncols)
    return epilogue(stress_change, direct_effect, load_rate, time_before)


def solution(mesh):
    in_specs = (
        P("rows", "cols"),
        P("cols", "rows", None),
        P("cols", "rows"),
        P("cols"),
        P(("rows", "cols")),
        P(("rows", "cols")),
        P(("rows", "cols")),
    )
    out_specs = (P(("rows", "cols"), None), P(("rows", "cols"), None))
    return jax.shard_map(
        per_device, mesh=mesh, in_specs=in_specs, out_specs=out_specs, check_vma=False
    )
```

```python
import functools

import jax
import jax.numpy as jnp
from jax import lax
from jax.experimental import pallas as pl
from jax.experimental.pallas import tpu as pltpu
from jax.sharding import PartitionSpec as P

BLOCK = 128
MESH = pl.DeviceIdType.MESH


def stress_kernel(nrows, ncols, groups, slip_ref, list_ref, count_ref, kernel_hbm, out_ref, pay_ref, kmat, gathered, dense_own,
                  landed, dense, sendbuf, slots, kload_sem, local_sem, g_send, g_recv, a_send, a_recv, r_send, r_recv, send_sem, recv_sem):
    me = lax.axis_index("cols")
    my_row = lax.axis_index("rows")
    share = out_ref.shape[0]
    per_group = ncols // groups
    here, list_here, patch = slip_ref.shape
    blocks = kmat.shape[1] // patch
    quarter = kmat.shape[0] // 4

    pay_ref[0] = slip_ref[...]
    for e in range(here):
        for b in range(list_here):
            live = my_row * list_here + b < count_ref[e]
            key = jnp.where(live, list_ref[e, b], -1)
            pay_ref[1, e, pl.ds(b, 1), :] = jnp.full((1, patch), key, jnp.int32).astype(jnp.float32)

    barrier = pltpu.get_barrier_semaphore()
    for k in range(1, nrows):
        peer = lax.rem(my_row + k, nrows)
        pl.semaphore_signal(barrier, inc=1, device_id=(peer, me), device_id_type=MESH)
    for k in range(1, ncols):
        peer = lax.rem(me + k, ncols)
        pl.semaphore_signal(barrier, inc=1, device_id=(my_row, peer), device_id_type=MESH)
    pl.semaphore_wait(barrier, nrows + ncols - 2)

    def entries(r):
        return pl.ds(pl.multiple_of(r * list_here, list_here), list_here)

    sends = []
    a2a_sends = []
    for peer in range(nrows):
        copy = pltpu.make_async_remote_copy(
            src_ref=pay_ref,
            dst_ref=gathered.at[:, :, entries(my_row)],
            send_sem=g_send.at[peer],
            recv_sem=g_recv.at[my_row],
            device_id=(peer, me),
            device_id_type=MESH,
        )

        @pl.when(my_row != peer)
        def _():
            copy.start()

        a2a_sends.append((None, peer, copy))
    local = pltpu.make_async_copy(pay_ref, gathered.at[:, :, entries(my_row)], local_sem)
    local.start()
    local.wait()
    for src in range(nrows):
        wait = pltpu.make_async_remote_copy(
            src_ref=pay_ref,
            dst_ref=gathered.at[:, :, entries(src)],
            send_sem=g_send.at[src],
            recv_sem=g_recv.at[src],
            device_id=(src, me),
            device_id_type=MESH,
        )

        @pl.when(my_row != src)
        def _():
            wait.wait_recv()

    total_blocks = dense_own.shape[1]
    lane = lax.broadcasted_iota(jnp.int32, (nrows * list_here, patch), 1)
    keys = [gathered[1, e].astype(jnp.int32) for e in range(here)]
    per_piece = patch // blocks
    for q in range(total_blocks // patch):
        for e in range(here):
            onehot = (keys[e] == lane + q * patch).astype(jnp.float32)
            dense_own[e, pl.ds(q * patch, patch), :] = lax.dot_general(
                onehot,
                gathered[0, e],
                (((0,), (0,)), ((), ())),
                precision=lax.Precision.HIGHEST,
                preferred_element_type=jnp.float32,
            )
        for i in range(per_piece):
            peer = q * per_piece + i
            copy = pltpu.make_async_remote_copy(
                src_ref=dense_own.at[:, pl.ds(peer * blocks, blocks)],
                dst_ref=landed.at[pl.ds(pl.multiple_of(me * here, here), here)],
                send_sem=a_send.at[peer],
                recv_sem=a_recv.at[me],
                device_id=(my_row, peer),
                device_id_type=MESH,
            )

            @pl.when(me != peer)
            def _():
                copy.start()

            a2a_sends.append((me, peer, copy))

    loads = []
    for q in range(4):
        load = pltpu.make_async_copy(
            kernel_hbm.at[pl.ds(q * quarter, quarter)], kmat.at[pl.ds(q * quarter, quarter)], kload_sem.at[q]
        )
        load.start()
        loads.append(load)

    def mine(c):
        return pl.ds(pl.multiple_of(c * blocks, blocks), blocks)

    def slot(c):
        return pl.ds(pl.multiple_of(c * here, here), here)

    local = pltpu.make_async_copy(dense_own.at[:, mine(me)], landed.at[slot(me)], local_sem)
    local.start()
    local.wait()
    for k in range(1, ncols):
        src = lax.rem(me + ncols - k, ncols)
        pltpu.make_async_remote_copy(
            src_ref=dense_own.at[:, mine(src)],
            dst_ref=landed.at[slot(src)],
            send_sem=a_send.at[src],
            recv_sem=a_recv.at[src],
            device_id=(my_row, src),
            device_id_type=MESH,
        ).wait_recv()

    relayout = []
    for j in range(blocks):
        copy = pltpu.make_async_copy(landed.at[:, j], dense.at[j], r_send.at[j])
        copy.start()
        relayout.append(copy)
    for copy in relayout:
        copy.wait()
    for load in loads:
        load.wait()

    rs_sends = []
    for g in range(groups):
        rows = pl.ds(g * per_group * share, per_group * share)
        part = None
        for j in range(blocks):
            term = lax.dot_general(
                kmat[rows, pl.ds(j * patch, patch)],
                dense[j],
                (((1,), (1,)), ((), ())),
                precision=lax.Precision.HIGH,
                preferred_element_type=jnp.float32,
            )
            part = term if part is None else part + term
        for j in range(per_group):
            dest = g * per_group + j
            sendbuf[dest] = part[j * share:(j + 1) * share]
            copy = pltpu.make_async_remote_copy(
                src_ref=sendbuf.at[dest],
                dst_ref=slots.at[me],
                send_sem=send_sem.at[dest],
                recv_sem=recv_sem.at[me],
                device_id=(my_row, dest),
                device_id_type=MESH,
            )

            @pl.when(me != dest)
            def _():
                copy.start()

            rs_sends.append((me, dest, copy))

    total = sendbuf[me]
    for k in range(1, ncols):
        src = lax.rem(me + ncols - k, ncols)
        pltpu.make_async_remote_copy(
            src_ref=sendbuf.at[src],
            dst_ref=slots.at[src],
            send_sem=send_sem.at[src],
            recv_sem=recv_sem.at[src],
            device_id=(my_row, src),
            device_id_type=MESH,
        ).wait_recv()
        total = total + slots[src]
    out_ref[...] = total
    for copy in sends:
        copy.wait_send()
    for own, dest, copy in a2a_sends + rs_sends:

        @pl.when((my_row if own is None else own) != dest)
        def _():
            copy.wait_send()


def stress_sum(kernel, slip_delta, block_list, live_count, nrows, ncols, groups=8):
    rows, sources = kernel.shape
    here, list_here, patch = slip_delta.shape
    events = ncols * here
    share = rows // ncols
    blocks = sources // patch
    return pl.pallas_call(
        functools.partial(stress_kernel, nrows, ncols, groups),
        out_shape=jax.ShapeDtypeStruct((share, events), jnp.float32),
        in_specs=[
            pl.BlockSpec(memory_space=pltpu.VMEM),
            pl.BlockSpec(memory_space=pltpu.SMEM),
            pl.BlockSpec(memory_space=pltpu.SMEM),
            pl.BlockSpec(memory_space=pl.ANY),
        ],
        out_specs=pl.BlockSpec(memory_space=pltpu.VMEM),
        scratch_shapes=[
            pltpu.VMEM((2, here, list_here, patch), jnp.float32),
            pltpu.VMEM((rows, sources), jnp.float32),
            pltpu.VMEM((2, here, nrows * list_here, patch), jnp.float32),
            pltpu.VMEM((here, ncols * blocks, patch), jnp.float32),
            pltpu.VMEM((events, blocks, patch), jnp.float32),
            pltpu.VMEM((blocks, events, patch), jnp.float32),
            pltpu.VMEM((ncols, share, events), jnp.float32),
            pltpu.VMEM((ncols, share, events), jnp.float32),
            pltpu.SemaphoreType.DMA((4,)),
            pltpu.SemaphoreType.DMA,
            pltpu.SemaphoreType.DMA((nrows,)),
            pltpu.SemaphoreType.DMA((nrows,)),
            pltpu.SemaphoreType.DMA((ncols,)),
            pltpu.SemaphoreType.DMA((ncols,)),
            pltpu.SemaphoreType.DMA((blocks,)),
            pltpu.SemaphoreType.DMA((blocks,)),
            pltpu.SemaphoreType.DMA((ncols,)),
            pltpu.SemaphoreType.DMA((ncols,)),
        ],
        compiler_params=pltpu.CompilerParams(collective_id=0, has_side_effects=True),
    )(slip_delta, block_list, live_count, kernel)


def epilogue_kernel(stress_ref, scale_ref, rate_ref, before_ref, out_ref, log_ref):
    stress = stress_ref[...]
    row = lax.broadcasted_iota(jnp.int32, stress.shape, 0)
    scale = jnp.ones_like(stress)
    rate = jnp.ones_like(stress)
    before = jnp.ones_like(stress)
    for i in range(stress.shape[0]):
        pick = row == i
        scale = jnp.where(pick, scale_ref[i], scale)
        rate = jnp.where(pick, rate_ref[i], rate)
        before = jnp.where(pick, before_ref[i], before)
    x = rate * before / scale
    u = jnp.exp(x)
    growth = jnp.where(u == 1.0, x, (u - 1.0) * x / jnp.log(u))
    out_ref[...] = stress
    log_ref[...] = jnp.log(scale / rate) + jnp.log(jnp.log1p(jnp.exp(-stress / scale) * growth))


def epilogue(stress, scale, rate, before):
    shape = jax.ShapeDtypeStruct(stress.shape, jnp.float32)
    return pl.pallas_call(
        epilogue_kernel,
        out_shape=(shape, shape),
        in_specs=[pl.BlockSpec(memory_space=pltpu.VMEM)] + [pl.BlockSpec(memory_space=pltpu.SMEM)] * 3,
        out_specs=(pl.BlockSpec(memory_space=pltpu.VMEM), pl.BlockSpec(memory_space=pltpu.VMEM)),
    )(stress, scale, rate, before)


def per_device(kernel, slip_delta, block_list, live_count, direct_effect, load_rate, time_before):
    nrows = lax.axis_size("rows")
    ncols = lax.axis_size("cols")
    stress_change = stress_sum(kernel, slip_delta, block_list, live_count, nrows, ncols)
    return epilogue(stress_change, direct_effect, load_rate, time_before)


def solution(mesh):
    in_specs = (
        P("rows", "cols"),
        P("cols", "rows", None),
        P("cols", "rows"),
        P("cols"),
        P(("rows", "cols")),
        P(("rows", "cols")),
        P(("rows", "cols")),
    )
    out_specs = (P(("rows", "cols"), None), P(("rows", "cols"), None))
    return jax.shard_map(
        per_device, mesh=mesh, in_specs=in_specs, out_specs=out_specs, check_vma=False
    )
```

```python
import functools

import jax
import jax.numpy as jnp
from jax import lax
from jax.experimental import pallas as pl
from jax.experimental.pallas import tpu as pltpu
from jax.sharding import PartitionSpec as P

BLOCK = 128
MESH = pl.DeviceIdType.MESH


def stress_kernel(nrows, ncols, groups, slip_ref, list_ref, count_ref, kernel_hbm, out_ref, pay_ref, kmat, gathered, dense_own,
                  landed, dense, sendbuf, slots, kload_sem, local_sem, g_send, g_recv, a_send, a_recv, r_send, r_recv, send_sem, recv_sem):
    me = lax.axis_index("cols")
    my_row = lax.axis_index("rows")
    share = out_ref.shape[0]
    per_group = ncols // groups
    here, list_here, patch = slip_ref.shape
    blocks = kmat.shape[1] // patch
    quarter = kmat.shape[0] // 4

    pay_ref[0] = slip_ref[...]
    for e in range(here):
        for b in range(list_here):
            live = my_row * list_here + b < count_ref[e]
            key = jnp.where(live, list_ref[e, b], -1)
            pay_ref[1, e, pl.ds(b, 1), :] = jnp.full((1, patch), key, jnp.int32).astype(jnp.float32)

    barrier = pltpu.get_barrier_semaphore()
    for k in range(1, nrows):
        peer = lax.rem(my_row + k, nrows)
        pl.semaphore_signal(barrier, inc=1, device_id=(peer, me), device_id_type=MESH)
    for k in range(1, ncols):
        peer = lax.rem(me + k, ncols)
        pl.semaphore_signal(barrier, inc=1, device_id=(my_row, peer), device_id_type=MESH)
    pl.semaphore_wait(barrier, nrows + ncols - 2)

    def entries(r):
        return pl.ds(pl.multiple_of(r * list_here, list_here), list_here)

    sends = []
    a2a_sends = []
    for peer in range(nrows):
        copy = pltpu.make_async_remote_copy(
            src_ref=pay_ref,
            dst_ref=gathered.at[:, :, entries(my_row)],
            send_sem=g_send.at[peer],
            recv_sem=g_recv.at[my_row],
            device_id=(peer, me),
            device_id_type=MESH,
        )

        @pl.when(my_row != peer)
        def _():
            copy.start()

        a2a_sends.append((None, peer, copy))
    local = pltpu.make_async_copy(pay_ref, gathered.at[:, :, entries(my_row)], local_sem)
    local.start()
    local.wait()
    for src in range(nrows):
        wait = pltpu.make_async_remote_copy(
            src_ref=pay_ref,
            dst_ref=gathered.at[:, :, entries(src)],
            send_sem=g_send.at[src],
            recv_sem=g_recv.at[src],
            device_id=(src, me),
            device_id_type=MESH,
        )

        @pl.when(my_row != src)
        def _():
            wait.wait_recv()

    total_blocks = dense_own.shape[1]
    lane = lax.broadcasted_iota(jnp.int32, (nrows * list_here, patch), 1)
    keys = [gathered[1, e].astype(jnp.int32) for e in range(here)]
    per_piece = patch // blocks
    for q in range(total_blocks // patch):
        for e in range(here):
            onehot = (keys[e] == lane + q * patch).astype(jnp.float32)
            dense_own[e, pl.ds(q * patch, patch), :] = lax.dot_general(
                onehot,
                gathered[0, e],
                (((0,), (0,)), ((), ())),
                precision=lax.Precision.HIGHEST,
                preferred_element_type=jnp.float32,
            )
        for i in range(per_piece):
            peer = q * per_piece + i
            copy = pltpu.make_async_remote_copy(
                src_ref=dense_own.at[:, pl.ds(peer * blocks, blocks)],
                dst_ref=landed.at[pl.ds(pl.multiple_of(me * here, here), here)],
                send_sem=a_send.at[peer],
                recv_sem=a_recv.at[me],
                device_id=(my_row, peer),
                device_id_type=MESH,
            )

            @pl.when(me != peer)
            def _():
                copy.start()

            a2a_sends.append((me, peer, copy))

    loads = []
    for q in range(4):
        load = pltpu.make_async_copy(
            kernel_hbm.at[pl.ds(q * quarter, quarter)], kmat.at[pl.ds(q * quarter, quarter)], kload_sem.at[q]
        )
        load.start()
        loads.append(load)

    def mine(c):
        return pl.ds(pl.multiple_of(c * blocks, blocks), blocks)

    def slot(c):
        return pl.ds(pl.multiple_of(c * here, here), here)

    local = pltpu.make_async_copy(dense_own.at[:, mine(me)], landed.at[slot(me)], local_sem)
    local.start()
    local.wait()
    for src in range(ncols):
        wait = pltpu.make_async_remote_copy(
            src_ref=dense_own.at[:, pl.ds(src * blocks, blocks)],
            dst_ref=landed.at[pl.ds(src * here, here)],
            send_sem=a_send.at[src],
            recv_sem=a_recv.at[src],
            device_id=(my_row, src),
            device_id_type=MESH,
        )

        @pl.when(me != src)
        def _():
            wait.wait_recv()

    relayout = []
    for j in range(blocks):
        copy = pltpu.make_async_copy(landed.at[:, j], dense.at[j], r_send.at[j])
        copy.start()
        relayout.append(copy)
    for copy in relayout:
        copy.wait()
    for load in loads:
        load.wait()

    rs_sends = []
    for g in range(groups):
        rows = pl.ds(g * per_group * share, per_group * share)
        part = None
        for j in range(blocks):
            term = lax.dot_general(
                kmat[rows, pl.ds(j * patch, patch)],
                dense[j],
                (((1,), (1,)), ((), ())),
                precision=lax.Precision.HIGH,
                preferred_element_type=jnp.float32,
            )
            part = term if part is None else part + term
        for j in range(per_group):
            dest = g * per_group + j
            sendbuf[dest] = part[j * share:(j + 1) * share]
            copy = pltpu.make_async_remote_copy(
                src_ref=sendbuf.at[dest],
                dst_ref=slots.at[me],
                send_sem=send_sem.at[dest],
                recv_sem=recv_sem.at[me],
                device_id=(my_row, dest),
                device_id_type=MESH,
            )

            @pl.when(me != dest)
            def _():
                copy.start()

            rs_sends.append((me, dest, copy))

    total = sendbuf[me]
    for k in range(1, ncols):
        src = lax.rem(me + ncols - k, ncols)
        pltpu.make_async_remote_copy(
            src_ref=sendbuf.at[src],
            dst_ref=slots.at[src],
            send_sem=send_sem.at[src],
            recv_sem=recv_sem.at[src],
            device_id=(my_row, src),
            device_id_type=MESH,
        ).wait_recv()
        total = total + slots[src]
    out_ref[...] = total
    for copy in sends:
        copy.wait_send()
    for own, dest, copy in a2a_sends + rs_sends:

        @pl.when((my_row if own is None else own) != dest)
        def _():
            copy.wait_send()


def stress_sum(kernel, slip_delta, block_list, live_count, nrows, ncols, groups=8):
    rows, sources = kernel.shape
    here, list_here, patch = slip_delta.shape
    events = ncols * here
    share = rows // ncols
    blocks = sources // patch
    return pl.pallas_call(
        functools.partial(stress_kernel, nrows, ncols, groups),
        out_shape=jax.ShapeDtypeStruct((share, events), jnp.float32),
        in_specs=[
            pl.BlockSpec(memory_space=pltpu.VMEM),
            pl.BlockSpec(memory_space=pltpu.SMEM),
            pl.BlockSpec(memory_space=pltpu.SMEM),
            pl.BlockSpec(memory_space=pl.ANY),
        ],
        out_specs=pl.BlockSpec(memory_space=pltpu.VMEM),
        scratch_shapes=[
            pltpu.VMEM((2, here, list_here, patch), jnp.float32),
            pltpu.VMEM((rows, sources), jnp.float32),
            pltpu.VMEM((2, here, nrows * list_here, patch), jnp.float32),
            pltpu.VMEM((here, ncols * blocks, patch), jnp.float32),
            pltpu.VMEM((events, blocks, patch), jnp.float32),
            pltpu.VMEM((blocks, events, patch), jnp.float32),
            pltpu.VMEM((ncols, share, events), jnp.float32),
            pltpu.VMEM((ncols, share, events), jnp.float32),
            pltpu.SemaphoreType.DMA((4,)),
            pltpu.SemaphoreType.DMA,
            pltpu.SemaphoreType.DMA((nrows,)),
            pltpu.SemaphoreType.DMA((nrows,)),
            pltpu.SemaphoreType.DMA((ncols,)),
            pltpu.SemaphoreType.DMA((ncols,)),
            pltpu.SemaphoreType.DMA((blocks,)),
            pltpu.SemaphoreType.DMA((blocks,)),
            pltpu.SemaphoreType.DMA((ncols,)),
            pltpu.SemaphoreType.DMA((ncols,)),
        ],
        compiler_params=pltpu.CompilerParams(collective_id=0, has_side_effects=True),
    )(slip_delta, block_list, live_count, kernel)


def epilogue_kernel(stress_ref, scale_ref, rate_ref, before_ref, out_ref, log_ref):
    stress = stress_ref[...]
    row = lax.broadcasted_iota(jnp.int32, stress.shape, 0)
    scale = jnp.ones_like(stress)
    rate = jnp.ones_like(stress)
    before = jnp.ones_like(stress)
    for i in range(stress.shape[0]):
        pick = row == i
        scale = jnp.where(pick, scale_ref[i], scale)
        rate = jnp.where(pick, rate_ref[i], rate)
        before = jnp.where(pick, before_ref[i], before)
    x = rate * before / scale
    u = jnp.exp(x)
    growth = jnp.where(u == 1.0, x, (u - 1.0) * x / jnp.log(u))
    out_ref[...] = stress
    log_ref[...] = jnp.log(scale / rate) + jnp.log(jnp.log1p(jnp.exp(-stress / scale) * growth))


def epilogue(stress, scale, rate, before):
    shape = jax.ShapeDtypeStruct(stress.shape, jnp.float32)
    return pl.pallas_call(
        epilogue_kernel,
        out_shape=(shape, shape),
        in_specs=[pl.BlockSpec(memory_space=pltpu.VMEM)] + [pl.BlockSpec(memory_space=pltpu.SMEM)] * 3,
        out_specs=(pl.BlockSpec(memory_space=pltpu.VMEM), pl.BlockSpec(memory_space=pltpu.VMEM)),
    )(stress, scale, rate, before)


def per_device(kernel, slip_delta, block_list, live_count, direct_effect, load_rate, time_before):
    nrows = lax.axis_size("rows")
    ncols = lax.axis_size("cols")
    stress_change = stress_sum(kernel, slip_delta, block_list, live_count, nrows, ncols)
    return epilogue(stress_change, direct_effect, load_rate, time_before)


def solution(mesh):
    in_specs = (
        P("rows", "cols"),
        P("cols", "rows", None),
        P("cols", "rows"),
        P("cols"),
        P(("rows", "cols")),
        P(("rows", "cols")),
        P(("rows", "cols")),
    )
    out_specs = (P(("rows", "cols"), None), P(("rows", "cols"), None))
    return jax.shard_map(
        per_device, mesh=mesh, in_specs=in_specs, out_specs=out_specs, check_vma=False
    )
```

```python
import functools

import jax
import jax.numpy as jnp
from jax import lax
from jax.experimental import pallas as pl
from jax.experimental.pallas import tpu as pltpu
from jax.sharding import PartitionSpec as P

BLOCK = 128
MESH = pl.DeviceIdType.MESH


def stress_kernel(nrows, ncols, groups, slip_ref, list_ref, count_ref, kernel_hbm, out_ref, pay_ref, kmat, gathered, dense_own,
                  landed, dense, sendbuf, slots, kload_sem, local_sem, g_send, g_recv, a_send, a_recv, r_send, r_recv, send_sem, recv_sem):
    me = lax.axis_index("cols")
    my_row = lax.axis_index("rows")
    share = out_ref.shape[0]
    per_group = ncols // groups
    here, list_here, patch = slip_ref.shape
    blocks = kmat.shape[1] // patch
    quarter = kmat.shape[0] // 4

    pay_ref[0] = slip_ref[...]
    for e in range(here):
        for b in range(list_here):
            live = my_row * list_here + b < count_ref[e]
            key = jnp.where(live, list_ref[e, b], -1)
            pay_ref[1, e, pl.ds(b, 1), :] = jnp.full((1, patch), key, jnp.int32).astype(jnp.float32)

    barrier = pltpu.get_barrier_semaphore()
    for peer in range(nrows):

        @pl.when(my_row != peer)
        def _():
            pl.semaphore_signal(barrier, inc=1, device_id=(peer, me), device_id_type=MESH)

    for peer in range(ncols):

        @pl.when(me != peer)
        def _():
            pl.semaphore_signal(barrier, inc=1, device_id=(my_row, peer), device_id_type=MESH)

    pl.semaphore_wait(barrier, nrows + ncols - 2)

    def entries(r):
        return pl.ds(pl.multiple_of(r * list_here, list_here), list_here)

    sends = []
    a2a_sends = []
    for peer in range(nrows):
        copy = pltpu.make_async_remote_copy(
            src_ref=pay_ref,
            dst_ref=gathered.at[:, :, entries(my_row)],
            send_sem=g_send.at[peer],
            recv_sem=g_recv.at[my_row],
            device_id=(peer, me),
            device_id_type=MESH,
        )

        @pl.when(my_row != peer)
        def _():
            copy.start()

        a2a_sends.append((None, peer, copy))
    local = pltpu.make_async_copy(pay_ref, gathered.at[:, :, entries(my_row)], local_sem)
    local.start()
    local.wait()
    for src in range(nrows):
        wait = pltpu.make_async_remote_copy(
            src_ref=pay_ref,
            dst_ref=gathered.at[:, :, entries(src)],
            send_sem=g_send.at[src],
            recv_sem=g_recv.at[src],
            device_id=(src, me),
            device_id_type=MESH,
        )

        @pl.when(my_row != src)
        def _():
            wait.wait_recv()

    total_blocks = dense_own.shape[1]
    lane = lax.broadcasted_iota(jnp.int32, (nrows * list_here, patch), 1)
    keys = [gathered[1, e].astype(jnp.int32) for e in range(here)]
    per_piece = patch // blocks
    for q in range(total_blocks // patch):
        for e in range(here):
            onehot = (keys[e] == lane + q * patch).astype(jnp.float32)
            dense_own[e, pl.ds(q * patch, patch), :] = lax.dot_general(
                onehot,
                gathered[0, e],
                (((0,), (0,)), ((), ())),
                precision=lax.Precision.HIGHEST,
                preferred_element_type=jnp.float32,
            )
        for i in range(per_piece):
            peer = q * per_piece + i
            copy = pltpu.make_async_remote_copy(
                src_ref=dense_own.at[:, pl.ds(peer * blocks, blocks)],
                dst_ref=landed.at[pl.ds(pl.multiple_of(me * here, here), here)],
                send_sem=a_send.at[peer],
                recv_sem=a_recv.at[me],
                device_id=(my_row, peer),
                device_id_type=MESH,
            )

            @pl.when(me != peer)
            def _():
                copy.start()

            a2a_sends.append((me, peer, copy))

    loads = []
    for q in range(4):
        load = pltpu.make_async_copy(
            kernel_hbm.at[pl.ds(q * quarter, quarter)], kmat.at[pl.ds(q * quarter, quarter)], kload_sem.at[q]
        )
        load.start()
        loads.append(load)

    def mine(c):
        return pl.ds(pl.multiple_of(c * blocks, blocks), blocks)

    def slot(c):
        return pl.ds(pl.multiple_of(c * here, here), here)

    local = pltpu.make_async_copy(dense_own.at[:, mine(me)], landed.at[slot(me)], local_sem)
    local.start()
    local.wait()
    for src in range(ncols):
        wait = pltpu.make_async_remote_copy(
            src_ref=dense_own.at[:, pl.ds(src * blocks, blocks)],
            dst_ref=landed.at[pl.ds(src * here, here)],
            send_sem=a_send.at[src],
            recv_sem=a_recv.at[src],
            device_id=(my_row, src),
            device_id_type=MESH,
        )

        @pl.when(me != src)
        def _():
            wait.wait_recv()

    relayout = []
    for j in range(blocks):
        copy = pltpu.make_async_copy(landed.at[:, j], dense.at[j], r_send.at[j])
        copy.start()
        relayout.append(copy)
    for copy in relayout:
        copy.wait()
    for load in loads:
        load.wait()

    rs_sends = []
    for g in range(groups):
        rows = pl.ds(g * per_group * share, per_group * share)
        part = None
        for j in range(blocks):
            term = lax.dot_general(
                kmat[rows, pl.ds(j * patch, patch)],
                dense[j],
                (((1,), (1,)), ((), ())),
                precision=lax.Precision.HIGH,
                preferred_element_type=jnp.float32,
            )
            part = term if part is None else part + term
        for j in range(per_group):
            dest = g * per_group + j
            sendbuf[dest] = part[j * share:(j + 1) * share]
            copy = pltpu.make_async_remote_copy(
                src_ref=sendbuf.at[dest],
                dst_ref=slots.at[me],
                send_sem=send_sem.at[dest],
                recv_sem=recv_sem.at[me],
                device_id=(my_row, dest),
                device_id_type=MESH,
            )

            @pl.when(me != dest)
            def _():
                copy.start()

            rs_sends.append((me, dest, copy))

    total = sendbuf[me]
    for k in range(1, ncols):
        src = lax.rem(me + ncols - k, ncols)
        pltpu.make_async_remote_copy(
            src_ref=sendbuf.at[src],
            dst_ref=slots.at[src],
            send_sem=send_sem.at[src],
            recv_sem=recv_sem.at[src],
            device_id=(my_row, src),
            device_id_type=MESH,
        ).wait_recv()
        total = total + slots[src]
    out_ref[...] = total
    for copy in sends:
        copy.wait_send()
    for own, dest, copy in a2a_sends + rs_sends:

        @pl.when((my_row if own is None else own) != dest)
        def _():
            copy.wait_send()


def stress_sum(kernel, slip_delta, block_list, live_count, nrows, ncols, groups=8):
    rows, sources = kernel.shape
    here, list_here, patch = slip_delta.shape
    events = ncols * here
    share = rows // ncols
    blocks = sources // patch
    return pl.pallas_call(
        functools.partial(stress_kernel, nrows, ncols, groups),
        out_shape=jax.ShapeDtypeStruct((share, events), jnp.float32),
        in_specs=[
            pl.BlockSpec(memory_space=pltpu.VMEM),
            pl.BlockSpec(memory_space=pltpu.SMEM),
            pl.BlockSpec(memory_space=pltpu.SMEM),
            pl.BlockSpec(memory_space=pl.ANY),
        ],
        out_specs=pl.BlockSpec(memory_space=pltpu.VMEM),
        scratch_shapes=[
            pltpu.VMEM((2, here, list_here, patch), jnp.float32),
            pltpu.VMEM((rows, sources), jnp.float32),
            pltpu.VMEM((2, here, nrows * list_here, patch), jnp.float32),
            pltpu.VMEM((here, ncols * blocks, patch), jnp.float32),
            pltpu.VMEM((events, blocks, patch), jnp.float32),
            pltpu.VMEM((blocks, events, patch), jnp.float32),
            pltpu.VMEM((ncols, share, events), jnp.float32),
            pltpu.VMEM((ncols, share, events), jnp.float32),
            pltpu.SemaphoreType.DMA((4,)),
            pltpu.SemaphoreType.DMA,
            pltpu.SemaphoreType.DMA((nrows,)),
            pltpu.SemaphoreType.DMA((nrows,)),
            pltpu.SemaphoreType.DMA((ncols,)),
            pltpu.SemaphoreType.DMA((ncols,)),
            pltpu.SemaphoreType.DMA((blocks,)),
            pltpu.SemaphoreType.DMA((blocks,)),
            pltpu.SemaphoreType.DMA((ncols,)),
            pltpu.SemaphoreType.DMA((ncols,)),
        ],
        compiler_params=pltpu.CompilerParams(collective_id=0, has_side_effects=True),
    )(slip_delta, block_list, live_count, kernel)


def epilogue_kernel(stress_ref, scale_ref, rate_ref, before_ref, out_ref, log_ref):
    stress = stress_ref[...]
    row = lax.broadcasted_iota(jnp.int32, stress.shape, 0)
    scale = jnp.ones_like(stress)
    rate = jnp.ones_like(stress)
    before = jnp.ones_like(stress)
    for i in range(stress.shape[0]):
        pick = row == i
        scale = jnp.where(pick, scale_ref[i], scale)
        rate = jnp.where(pick, rate_ref[i], rate)
        before = jnp.where(pick, before_ref[i], before)
    x = rate * before / scale
    u = jnp.exp(x)
    growth = jnp.where(u == 1.0, x, (u - 1.0) * x / jnp.log(u))
    out_ref[...] = stress
    log_ref[...] = jnp.log(scale / rate) + jnp.log(jnp.log1p(jnp.exp(-stress / scale) * growth))


def epilogue(stress, scale, rate, before):
    shape = jax.ShapeDtypeStruct(stress.shape, jnp.float32)
    return pl.pallas_call(
        epilogue_kernel,
        out_shape=(shape, shape),
        in_specs=[pl.BlockSpec(memory_space=pltpu.VMEM)] + [pl.BlockSpec(memory_space=pltpu.SMEM)] * 3,
        out_specs=(pl.BlockSpec(memory_space=pltpu.VMEM), pl.BlockSpec(memory_space=pltpu.VMEM)),
    )(stress, scale, rate, before)


def per_device(kernel, slip_delta, block_list, live_count, direct_effect, load_rate, time_before):
    nrows = lax.axis_size("rows")
    ncols = lax.axis_size("cols")
    stress_change = stress_sum(kernel, slip_delta, block_list, live_count, nrows, ncols)
    return epilogue(stress_change, direct_effect, load_rate, time_before)


def solution(mesh):
    in_specs = (
        P("rows", "cols"),
        P("cols", "rows", None),
        P("cols", "rows"),
        P("cols"),
        P(("rows", "cols")),
        P(("rows", "cols")),
        P(("rows", "cols")),
    )
    out_specs = (P(("rows", "cols"), None), P(("rows", "cols"), None))
    return jax.shard_map(
        per_device, mesh=mesh, in_specs=in_specs, out_specs=out_specs, check_vma=False
    )
```
